512 devices in a mesh: board: 8 (over y), sub: 64 (over z, x, core).
Axes of the slice: x: 4, y: 8, z: 8, core: 2. Of those that a mesh axis runs over, the one named last changes fastest.
Arguments:
- rhs: float32 [8, 32, 16384], P('board', None, 'sub')
- schur: float32 [8, 49152, 768], P('board', 'sub'), as said below
- block_list: int32 [8, 384], P('board', 'sub'), may hold values from 0 to 127, as said below
- pad_rows: int32 [8, 4096], P('board', 'sub'), may hold values from 0 to 255, as said below
- pad_cond: float32 [8, 4096], P('board', 'sub'), may hold values from 0.5 to 2
- sink: float32 [8, 16384], P('board', 'sub'), may hold values from 0.2 to 2
- precond: float32 [8, 16384], P('board', 'sub'), may hold values from 0.3 to 1
Outputs:
- solution: float32 [8, 32, 16384], P('board', None, 'sub')
- residual: float32 [8, 32, 16384], P('board', None, 'sub')
The draws below stay inside these ranges and needn't reach their ends.
Inputs may be any that keep to these rules, and one draw needn't show every extreme that they name: `block_list`: every entry of a subdomain s's list is a block owned by a subdomain at most 3 away from s on the same board; the entries of one list are different and rising, and include all blocks that s owns. `pad_rows`: A subdomain's pad rows are different and rising, and include its first and last owned row. `schur`: each Schur block is symmetric and positive definite.
All inputs are finite; a program needn't handle non-finite values.
Results may differ from the reference program's by a relative error of at most 0.0003.
Values sent between devices are 32-bit elements; how exact they have to be, the bound alone decides.
A program may use at most 64 MiB of HBM per device.

```python
import math
import jax
import jax.numpy as jnp
from jax import lax

OWN = 2
BR = 128
LB = 6
REACH = 3
NC = 32
PADS = 64
ITERS = 2
NI = 768
NBLK = 128
GROWS = 16384
N_BOARD = 8
N_SUB = 64


def draw_rhs(key, part):
    first = jax.random.fold_in(key, 0)
    third = jax.random.fold_in(key, 2)
    fourth = jax.random.fold_in(key, 3)
    rows = jnp.arange(GROWS, dtype=jnp.float32)
    ramp = 1.0 + 2.0 * rows / max(GROWS - 1, 1)
    rough = jnp.exp(jax.random.uniform(third, (N_BOARD, 1, GROWS), jnp.float32, -0.55, 0.55))
    case_scale = jnp.exp(jax.random.uniform(fourth, (1, NC, 1), jnp.float32, math.log(0.3), math.log(3.0)))
    base = jnp.clip(jax.random.normal(first, (N_BOARD, NC, GROWS), jnp.float32), -6.0, 6.0)
    return (base * ramp[None, None, :] * rough * case_scale).astype(jnp.float32)


def draw_schur(key, part):
    count = N_BOARD * N_SUB
    first, second = jax.random.split(key, 2)
    raw = jax.random.uniform(first, (count, NI, NI), jnp.float32, -1.7320508, 1.7320508)
    mixed = (raw + jnp.swapaxes(raw, 1, 2)) * (0.45 / math.sqrt(2.0 * NI))
    diagonal = jax.random.uniform(second, (count, NI), jnp.float32, 1.5, 3.0)
    rows = jnp.arange(NI, dtype=jnp.int32)
    on_diag = (rows[:, None] == rows[None, :]).astype(jnp.float32)
    matrix = mixed + on_diag[None, :, :] * diagonal[:, :, None]
    return matrix.reshape(N_BOARD, N_SUB * NI, NI).astype(jnp.float32)


def draw_block_list(key, part):
    count = N_BOARD * N_SUB
    domain = jnp.arange(count, dtype=jnp.int32) % N_SUB
    blocks = jnp.arange(NBLK, dtype=jnp.int32)
    owner = blocks // OWN
    distance = jnp.abs(owner[None, :] - domain[:, None])
    raw = jax.random.randint(jax.random.fold_in(key, 11), (count, NBLK), 0, 1 << 16)
    score = raw * NBLK + blocks[None, :]
    score = jnp.where(distance == 0, (1 << 26) + blocks[None, :], score)
    score = jnp.where(distance <= REACH, score, -1 - blocks[None, :])
    chosen = jax.lax.top_k(score, LB)[1].astype(jnp.int32)
    chosen = jnp.sort(chosen, axis=1)
    return chosen.reshape(N_BOARD, N_SUB * LB)


def draw_pad_rows(key, part):
    count = N_BOARD * N_SUB
    owned = OWN * BR
    rows = jnp.arange(owned, dtype=jnp.int32)
    raw = jax.random.randint(jax.random.fold_in(key, 23), (count, owned), 0, 1 << 16)
    score = raw * owned + rows[None, :]
    ends = jnp.logical_or(rows == 0, rows == owned - 1)
    score = jnp.where(ends[None, :], (1 << 28) + rows[None, :], score)
    chosen = jax.lax.top_k(score, PADS)[1].astype(jnp.int32)
    chosen = jnp.sort(chosen, axis=1)
    return chosen.reshape(N_BOARD, N_SUB * PADS)


def block_scale(stream_key, shape, cuts, least, top_value):
    def one(position, blocks):
        steps = jax.random.uniform(jax.random.fold_in(jax.random.fold_in(stream_key, 6), position), (blocks,), jnp.float32, least / len(cuts), top_value / len(cuts))
        return jnp.repeat(jnp.exp(steps), shape[position] // blocks).reshape((-1,) + (1,) * (len(shape) - position - 1))

    loudness = one(*cuts[0])
    for cut in cuts[1:]:
        loudness = loudness * one(*cut)
    return loudness


def setup_inputs(seed: int = 0) -> dict:
    key_of = jax.random.split(jax.random.key(seed), 8)
    rhs = draw_rhs(jax.random.fold_in(key_of[7], 71), 0)
    schur = draw_schur(jax.random.fold_in(key_of[7], 71), 0)
    block_list = draw_block_list(jax.random.fold_in(key_of[7], 71), 0)
    pad_rows = draw_pad_rows(jax.random.fold_in(key_of[7], 71), 0)
    pad_cond = jnp.clip(jnp.exp(math.log(2.0) - 1.3862944 * jax.random.uniform(key_of[4], (N_BOARD, N_SUB * PADS), jnp.float32) ** block_scale(key_of[4], (N_BOARD, N_SUB * PADS), ((0, 8), (1, 64)), -0.2, 0.2)), 0.5, 2.0)
    sink = jnp.clip(jnp.exp(math.log(2.0) - 2.3025851 * jax.random.uniform(key_of[5], (N_BOARD, GROWS), jnp.float32) ** block_scale(key_of[5], (N_BOARD, GROWS), ((0, 8), (1, 64)), -0.2, 0.2)), 0.2, 2.0)
    precond = jnp.clip(jnp.exp(math.log(1.0) - 1.2039728 * jax.random.uniform(key_of[6], (N_BOARD, GROWS), jnp.float32) ** block_scale(key_of[6], (N_BOARD, GROWS), ((0, 8), (1, 64)), -0.2, 0.2)), 0.3, 1.0)
    return dict(rhs=rhs, schur=schur, block_list=block_list, pad_rows=pad_rows, pad_cond=pad_cond, sink=sink, precond=precond)


def apply_operator(direction, schur, block_list, pad_rows, pad_cond, sink):
    mats = schur.reshape(N_BOARD * N_SUB, NI, NI)
    lists = block_list.reshape(N_BOARD * N_SUB, LB)
    start = jnp.zeros((N_BOARD, NC, NBLK, BR), jnp.float32)

    def one_domain(total, item):
        number, matrix, block_ids = item
        board_id = number // N_SUB
        blocks = lax.dynamic_index_in_dim(direction, board_id, 0, keepdims=False).reshape(NC, NBLK, BR)
        picked = jnp.take(blocks, block_ids, axis=1).reshape(NC, NI)
        product = jnp.dot(picked, matrix, precision=lax.Precision.HIGHEST).reshape(NC, LB, BR)
        current = lax.dynamic_index_in_dim(total, board_id, 0, keepdims=False)
        current = current.at[:, block_ids].add(product)
        return lax.dynamic_update_index_in_dim(total, current, board_id, 0), None

    numbers = jnp.arange(N_BOARD * N_SUB, dtype=jnp.int32)
    total, unused = lax.scan(one_domain, start, (numbers, mats, lists))
    result = total.reshape(N_BOARD, NC, GROWS)
    offsets = (jnp.arange(N_SUB, dtype=jnp.int32) * (OWN * BR))[None, :, None]
    rows_all = (pad_rows.reshape(N_BOARD, N_SUB, PADS) + offsets).reshape(N_BOARD, N_SUB * PADS)
    pad_values = jnp.take_along_axis(direction, rows_all[:, None, :], axis=2)
    partner = jnp.arange(N_BOARD, dtype=jnp.int32) ^ 1
    mean_cond = 0.5 * (pad_cond + pad_cond[partner])
    coupling = mean_cond[:, None, :] * (pad_values - pad_values[partner])
    board_ids = jnp.arange(N_BOARD, dtype=jnp.int32)[:, None, None]
    case_ids = jnp.arange(NC, dtype=jnp.int32)[None, :, None]
    result = result.at[board_ids, case_ids, rows_all[:, None, :]].add(coupling)
    return result + sink[:, None, :] * direction


def case_sums(left, right):
    return jnp.sum(left * right, axis=(0, 2))


def reference(rhs, schur, block_list, pad_rows, pad_cond, sink, precond):
    scaling = precond[:, None, :]
    solution = jnp.zeros_like(rhs)
    residual = rhs
    precon = scaling * residual
    direction = precon
    norm_now = case_sums(residual, precon)
    for iteration in range(ITERS):
        image = apply_operator(direction, schur, block_list, pad_rows, pad_cond, sink)
        alpha = norm_now / case_sums(direction, image)
        solution = solution + alpha[None, :, None] * direction
        residual = residual - alpha[None, :, None] * image
        if iteration < ITERS - 1:
            precon = scaling * residual
            fresh = case_sums(residual, precon)
            direction = precon + (fresh / norm_now)[None, :, None] * direction
            norm_now = fresh
    return solution, residual
```

```python
import functools

import jax
import jax.numpy as jnp
from jax import lax
from jax.experimental import pallas as pl
from jax.experimental.pallas import tpu as pltpu
from jax.sharding import PartitionSpec as P

BR = 128
REACH = 3
OFFSETS = (3, -3, 2, -2, 1, -1)
F32 = jnp.float32
BF16 = jnp.bfloat16


def split(value):
    high = value.astype(BF16)
    low = (value - high.astype(F32)).astype(BF16)
    return high, low


def kernel(
    n_board, n_sub,
    rhs, schur, blocks, pad_rows, pad_cond, sink, precond,
    x_out, r_out,
    b_own, s_full, s_high, s_low, one_hot, pad_out, pad_in, pad_keep,
    halo, prod, parts, back, image_own, group_a, group_b,
    load_sem, halo_send, halo_recv, back_send, back_recv, pad_send, pad_recv,
    a_send, a_recv, b_send, b_recv,
):
    me_b = lax.axis_index("board")
    me_s = lax.axis_index("sub")
    core = lax.rem(me_s, 2)
    chip = lax.div(me_s, 2)
    n_a, n_chip = 2 * n_board, n_sub // 2
    a_id = me_b * 2 + core
    partner = me_b + 1 - 2 * lax.rem(me_b, 2)
    touched = blocks.shape[1]
    inner = schur.shape[1]

    def near(offset):
        return (me_b, lax.rem(me_s + offset + n_sub, n_sub))

    def in_a(step):
        other = lax.rem(a_id + step, n_a)
        return (lax.div(other, 2), 2 * chip + lax.rem(other, 2))

    def in_b(step):
        return (me_b, 2 * lax.rem(chip + step, n_chip) + core)

    loads = [
        pltpu.make_async_copy(rhs.at[0, :, pl.ds(BR * i, BR)], b_own.at[i], load_sem.at[i])
        for i in range(2)
    ]
    rows = inner // 6
    for i in range(6):
        cut = pl.ds(rows * i, rows)
        loads.append(pltpu.make_async_copy(schur.at[0, cut], s_full.at[cut], load_sem.at[2 + i]))
    for load in loads:
        load.start()

    barrier = pltpu.get_barrier_semaphore()

    def greet(device):
        pl.semaphore_signal(barrier, inc=1, device_id=device, device_id_type=pl.DeviceIdType.MESH)

    for offset in (3, -3):
        greet(near(offset))
    greet((me_b, lax.rem(me_s + 2 * core - 1 + n_sub, n_sub)))
    for step in range(1, n_a):
        greet(in_a(step))
    for step in range(1, n_chip):
        greet(in_b(step))

    loads[0].wait()
    loads[1].wait()
    scale = [precond[0:1, BR * i : BR * (i + 1)] for i in range(2)]
    leak = [sink[0:1, BR * i : BR * (i + 1)] for i in range(2)]
    for i in range(2):
        halo[0, 2 * REACH + i] = scale[i] * b_own[i]
    pad_out[...] = jnp.zeros_like(pad_out)
    prod[touched] = jnp.zeros_like(prod[touched])
    n_pads = pad_rows.shape[1]
    row_ids = lax.broadcasted_iota(jnp.int32, (2 * BR, n_pads), 0)
    one_hot[...] = jnp.zeros_like(one_hot)
    one_hot[:, :n_pads] = jnp.where(row_ids == pad_rows[...], 1.0, 0.0).astype(BF16)

    def pads_of(slot):
        high, low = split(jnp.concatenate([halo[slot, 2 * REACH], halo[slot, 2 * REACH + 1]], axis=1))
        both = jnp.dot(jnp.concatenate([high, low], axis=0), one_hot[...], preferred_element_type=F32)
        return both[:32] + both[32:]

    own_pads = pads_of(0)
    pad_out[0, :32] = own_pads
    pad_out[0, 32:33, :n_pads] = pad_cond[...]
    last = 2 * (2 * REACH + 1) - 1
    index = [jnp.clip(blocks[0, j] - (me_s - REACH) * 2, 0, last) for j in range(touched)]
    inverse = []
    for k in range(2 * (2 * REACH + 1)):
        where = jnp.int32(touched)
        for j in range(touched):
            where = jnp.where(index[j] == k, j, where)
        inverse.append(where)

    pl.semaphore_wait(barrier, 3 + n_a - 1 + n_chip - 1)

    sent = []

    def send(source, target, send_sem, recv_sem, device):
        copy = pltpu.make_async_remote_copy(
            src_ref=source, dst_ref=target, send_sem=send_sem, recv_sem=recv_sem,
            device_id=device, device_id_type=pl.DeviceIdType.MESH,
        )
        copy.start()
        sent.append(copy)
        return copy

    def send_halo(slot):
        copies = []
        for n, offset in enumerate(OFFSETS):
            copies.append(send(
                halo.at[slot, pl.ds(2 * REACH, 2)], halo.at[slot, pl.ds(2 * (REACH - offset), 2)],
                halo_send.at[slot, n], halo_recv.at[slot, n], near(offset)))
        copies.append(send(pad_out.at[slot], pad_in.at[slot], pad_send.at[slot], pad_recv.at[slot], (partner, me_s)))
        return copies

    def send_back(slot):
        copies = []
        for n, offset in enumerate(OFFSETS):
            copies.append(send(
                parts.at[slot, pl.ds(2 * (REACH + offset), 2)], back.at[slot, n],
                back_send.at[slot, n], back_recv.at[slot, n], near(offset)))
        return copies

    def apply(slot):
        picked = [halo[slot, index[j]] for j in range(touched)]
        splits = [split(block) for block in picked]
        high = jnp.concatenate([pair[0] for pair in splits], axis=1)
        low = jnp.concatenate([pair[1] for pair in splits], axis=1)
        both = jnp.dot(jnp.concatenate([high, low], axis=0), s_high[...], preferred_element_type=F32)
        product = both[:32] + both[32:] + jnp.dot(high, s_low[...], preferred_element_type=F32)
        return picked, [product[:, BR * j : BR * (j + 1)] for j in range(touched)]

    def put_parts(slot, product):
        for j in range(touched):
            prod[j] = product[j]
        for k in range(2 * (2 * REACH + 1)):
            parts[slot, k] = prod[inverse[k]]

    def collect(slot, copies, coupling):
        high, low = split(coupling)
        both = lax.dot_general(
            jnp.concatenate([high, low], axis=0), one_hot[...], (((1,), (1,)), ((), ())), preferred_element_type=F32)
        spread = both[:32] + both[32:]
        for copy in copies:
            copy.wait_recv()
        result = []
        for i in range(2):
            total = parts[slot, 2 * REACH + i]
            for n in range(len(OFFSETS)):
                total = total + back[slot, n, i]
            total = total + spread[:, BR * i : BR * (i + 1)]
            result.append(total + leak[i] * halo[slot, 2 * REACH + i])
        return result

    def start_sum(slot, terms):
        stacked = jnp.concatenate(terms, axis=0)
        row = jnp.sum(stacked.T, axis=0, keepdims=True)
        group_a[slot, a_id] = row
        return [
            send(group_a.at[slot, a_id], group_a.at[slot, a_id],
                 a_send.at[slot, step - 1], a_recv.at[slot, step - 1], in_a(step))
            for step in range(1, n_a)
        ]

    def mid_sum(slot, copies):
        for copy in copies:
            copy.wait_recv()
        group_b[slot, chip] = jnp.sum(group_a[slot], axis=0)
        return [
            send(group_b.at[slot, chip], group_b.at[slot, chip],
                 b_send.at[slot, step - 1], b_recv.at[slot, step - 1], in_b(step))
            for step in range(1, n_chip)
        ]

    def end_sum(slot, copies):
        for copy in copies:
            copy.wait_recv()
        row = jnp.sum(group_b[slot], axis=0)
        return jnp.broadcast_to(row, (128, 128)).T

    halo_copies = send_halo(0)
    for i in range(6):
        loads[2 + i].wait()
        cut = pl.ds(rows * i, rows)
        high, low = split(s_full[cut])
        s_high[cut] = high
        s_low[cut] = low
    halo_copies[-1].wait_recv()
    mean_cond = 0.5 * (pad_out[0, 32:33] + pad_in[0, 32:33])
    coupling0 = mean_cond * (own_pads - pad_in[0, :32])
    for copy in halo_copies[:-1]:
        copy.wait_recv()
    picked0, product0 = apply(0)
    put_parts(0, product0)
    back_copies = send_back(0)
    curve = own_pads * coupling0
    start = jnp.zeros_like(curve)
    for j in range(touched):
        curve = curve + picked0[j] * product0[j]
    for i in range(2):
        direction = halo[0, 2 * REACH + i]
        curve = curve + leak[i] * direction * direction
        start = start + b_own[i] * direction
    sums = start_sum(0, [start, curve, jnp.zeros_like(curve), jnp.zeros_like(curve)])

    image = collect(0, back_copies, coupling0)
    for i in range(2):
        image_own[i] = image[i]
        halo[1, 2 * REACH + i] = scale[i] * image[i]
    own_pads1 = pads_of(1)
    pad_out[1, :32] = own_pads1
    halo_copies = send_halo(1)
    sums = mid_sum(0, sums)
    for copy in halo_copies:
        copy.wait_recv()
    picked1, product1 = apply(1)
    put_parts(1, product1)
    coupling1 = mean_cond * (own_pads1 - pad_in[1, :32])
    total = end_sum(0, sums)
    norm0, curve0 = total[:32], total[32:64]
    alpha0 = norm0 / curve0
    pads_z = own_pads - alpha0 * own_pads1
    curve = pads_z * (coupling0 - alpha0 * coupling1)
    for j in range(touched):
        curve = curve + (picked0[j] - alpha0 * picked1[j]) * (product0[j] - alpha0 * product1[j])
    fresh = jnp.zeros_like(curve)
    cross = jnp.zeros_like(curve)
    for i in range(2):
        residual = b_own[i] - alpha0 * image_own[i]
        z = scale[i] * residual
        fresh = fresh + residual * z
        cross = cross + z * image_own[i]
        curve = curve + leak[i] * z * z
    sums = start_sum(1, [fresh, curve, cross, jnp.zeros_like(curve)])
    back_copies = send_back(1)
    sums = mid_sum(1, sums)
    image_u = collect(1, back_copies, coupling1)
    total = end_sum(1, sums)
    norm1, zaz, zap = total[:32], total[32:64], total[64:96]
    beta = norm1 / norm0
    alpha1 = norm1 / (zaz + beta * (2.0 * zap + beta * curve0))
    for i in range(2):
        old = halo[0, 2 * REACH + i]
        residual = b_own[i] - alpha0 * image_own[i]
        direction = scale[i] * residual + beta * old
        image1 = (image_own[i] - alpha0 * image_u[i]) + beta * image_own[i]
        x_out[0, :, BR * i : BR * (i + 1)] = alpha0 * old + alpha1 * direction
        r_out[0, :, BR * i : BR * (i + 1)] = residual - alpha1 * image1
    for copy in sent:
        copy.wait_send()


def solution(mesh):
    n_board, n_sub = mesh.shape["board"], mesh.shape["sub"]
    vmem = pl.BlockSpec(memory_space=pltpu.VMEM)
    anywhere = pl.BlockSpec(memory_space=pl.ANY)
    smem = pl.BlockSpec(memory_space=pltpu.SMEM)

    def on_device(rhs, schur, block_list, pad_rows, pad_cond, sink, precond):
        cases, owned = rhs.shape[1:]
        inner = schur.shape[1]
        n_off = len(OFFSETS)
        span = 2 * (2 * REACH + 1)
        dma = pltpu.SemaphoreType.DMA
        out = jax.ShapeDtypeStruct(rhs.shape, F32)
        return pl.pallas_call(
            functools.partial(kernel, n_board, n_sub),
            out_shape=(out, out),
            in_specs=[anywhere, anywhere, smem, vmem, vmem, vmem, vmem],
            out_specs=(vmem, vmem),
            scratch_shapes=[
                pltpu.VMEM((2, cases, BR), F32),
                pltpu.VMEM((inner, inner), F32),
                pltpu.VMEM((inner, inner), BF16),
                pltpu.VMEM((inner, inner), BF16),
                pltpu.VMEM((owned, BR), BF16),
                pltpu.VMEM((2, cases + 8, BR), F32),
                pltpu.VMEM((2, cases + 8, BR), F32),
                pltpu.VMEM((cases, BR), F32),
                pltpu.VMEM((2, span, cases, BR), F32),
                pltpu.VMEM((block_list.shape[1] + 1, cases, BR), F32),
                pltpu.VMEM((2, span, cases, BR), F32),
                pltpu.VMEM((2, n_off, 2, cases, BR), F32),
                pltpu.VMEM((2, cases, BR), F32),
                pltpu.VMEM((2, 2 * n_board, 1, 128), F32),
                pltpu.VMEM((2, n_sub // 2, 1, 128), F32),
                dma((8,)),
                dma((2, n_off)), dma((2, n_off)),
                dma((2, n_off)), dma((2, n_off)),
                dma((2,)), dma((2,)),
                dma((2, 2 * n_board - 1)), dma((2, 2 * n_board - 1)),
                dma((2, n_sub // 2 - 1)), dma((2, n_sub // 2 - 1)),
            ],
            compiler_params=pltpu.CompilerParams(
                collective_id=0, has_side_effects=True, vmem_limit_bytes=32 * 1024 * 1024
            ),
        )(rhs, schur, block_list, pad_rows, pad_cond, sink, precond)

    row = P("board", "sub")
    return jax.shard_map(
        on_device,
        mesh=mesh,
        in_specs=(P("board", None, "sub"), P("board", "sub", None), row, row, row, row, row),
        out_specs=(P("board", None, "sub"), P("board", None, "sub")),
        check_vma=False,
    )
```

```python
import functools

import jax
import jax.numpy as jnp
from jax import lax
from jax.experimental import pallas as pl
from jax.experimental.pallas import tpu as pltpu
from jax.sharding import PartitionSpec as P

BR = 128
REACH = 3
OFFSETS = (3, -3, 2, -2, 1, -1)
F32 = jnp.float32
BF16 = jnp.bfloat16


def split(value):
    high = value.astype(BF16)
    low = (value - high.astype(F32)).astype(BF16)
    return high, low


def kernel(
    n_board, n_sub,
    rhs, schur, blocks_in, pad_rows_in, pad_cond_in, sink_in, precond_in,
    x_out, r_out,
    blocks, pad_rows, pad_cond, sink, precond,
    b_own, s_full, s_high, s_low, one_hot, pad_out, pad_in,
    halo, prod, parts, back, image_own, group_a, group_b,
    load_sem, halo_send, halo_recv, back_send, back_recv, pad_send, pad_recv,
    a_send, a_recv, b_send, b_recv,
):
    me_b = lax.axis_index("board")
    me_s = lax.axis_index("sub")
    core = lax.rem(me_s, 2)
    chip = lax.div(me_s, 2)
    n_a, n_chip = 2 * n_board, n_sub // 2
    a_id = me_b * 2 + core
    partner = me_b + 1 - 2 * lax.rem(me_b, 2)
    touched = blocks.shape[1]
    inner = schur.shape[1]

    def near(offset):
        return (me_b, lax.rem(me_s + offset + n_sub, n_sub))

    def in_a(step):
        other = lax.rem(a_id + step, n_a)
        return (lax.div(other, 2), 2 * chip + lax.rem(other, 2))

    def in_b(step):
        return (me_b, 2 * lax.rem(chip + step, n_chip) + core)

    loads = [
        pltpu.make_async_copy(rhs.at[0, :, pl.ds(BR * i, BR)], b_own.at[i], load_sem.at[i])
        for i in range(2)
    ]
    small = ((precond_in, precond), (pad_rows_in, pad_rows), (blocks_in, blocks), (pad_cond_in, pad_cond), (sink_in, sink))
    for i, (source, target) in enumerate(small):
        loads.append(pltpu.make_async_copy(source, target, load_sem.at[2 + i]))
    rows = inner // 6
    for i in range(6):
        cut = pl.ds(rows * i, rows)
        loads.append(pltpu.make_async_copy(schur.at[0, cut], s_full.at[cut], load_sem.at[7 + i]))
    for load in loads:
        load.start()

    barrier = pltpu.get_barrier_semaphore()

    def greet(device):
        pl.semaphore_signal(barrier, inc=1, device_id=device, device_id_type=pl.DeviceIdType.MESH)

    for offset in (3, -3):
        greet(near(offset))
    greet((me_b, lax.rem(me_s + 2 * core - 1 + n_sub, n_sub)))
    for step in range(1, n_a):
        greet(in_a(step))
    for step in range(1, n_chip):
        greet(in_b(step))

    for load in loads[:7]:
        load.wait()
    scale = [precond[0:1, BR * i : BR * (i + 1)] for i in range(2)]
    leak = [sink[0:1, BR * i : BR * (i + 1)] for i in range(2)]
    for i in range(2):
        halo[0, 2 * REACH + i] = scale[i] * b_own[i]
    pad_out[...] = jnp.zeros_like(pad_out)
    prod[touched] = jnp.zeros_like(prod[touched])
    n_pads = pad_rows.shape[1]
    row_ids = lax.broadcasted_iota(jnp.int32, (2 * BR, n_pads), 0)
    one_hot[...] = jnp.zeros_like(one_hot)
    one_hot[:, :n_pads] = jnp.where(row_ids == pad_rows[...], 1.0, 0.0).astype(BF16)

    def pads_of(slot):
        high, low = split(jnp.concatenate([halo[slot, 2 * REACH], halo[slot, 2 * REACH + 1]], axis=1))
        both = jnp.dot(jnp.concatenate([high, low], axis=0), one_hot[...], preferred_element_type=F32)
        return both[:32] + both[32:]

    own_pads = pads_of(0)
    pad_out[0, :32] = own_pads
    pad_out[0, 32:33, :n_pads] = pad_cond[...]
    last = 2 * (2 * REACH + 1) - 1
    index = [jnp.clip(blocks[0, j] - (me_s - REACH) * 2, 0, last) for j in range(touched)]
    inverse = []
    for k in range(2 * (2 * REACH + 1)):
        where = jnp.int32(touched)
        for j in range(touched):
            where = jnp.where(index[j] == k, j, where)
        inverse.append(where)

    pl.semaphore_wait(barrier, 3 + n_a - 1 + n_chip - 1)

    sent = []

    def send(source, target, send_sem, recv_sem, device):
        copy = pltpu.make_async_remote_copy(
            src_ref=source, dst_ref=target, send_sem=send_sem, recv_sem=recv_sem,
            device_id=device, device_id_type=pl.DeviceIdType.MESH,
        )
        copy.start()
        sent.append(copy)
        return copy

    def send_halo(slot):
        copies = []
        for n, offset in enumerate(OFFSETS):
            copies.append(send(
                halo.at[slot, pl.ds(2 * REACH, 2)], halo.at[slot, pl.ds(2 * (REACH - offset), 2)],
                halo_send.at[slot, n], halo_recv.at[slot, n], near(offset)))
        copies.append(send(pad_out.at[slot], pad_in.at[slot], pad_send.at[slot], pad_recv.at[slot], (partner, me_s)))
        return copies

    def send_back(slot):
        copies = []
        for n, offset in enumerate(OFFSETS):
            copies.append(send(
                parts.at[slot, pl.ds(2 * (REACH + offset), 2)], back.at[slot, n],
                back_send.at[slot, n], back_recv.at[slot, n], near(offset)))
        return copies

    def apply(slot):
        picked = [halo[slot, index[j]] for j in range(touched)]
        splits = [split(block) for block in picked]
        high = jnp.concatenate([pair[0] for pair in splits], axis=1)
        low = jnp.concatenate([pair[1] for pair in splits], axis=1)
        both = jnp.dot(jnp.concatenate([high, low], axis=0), s_high[...], preferred_element_type=F32)
        product = both[:32] + both[32:] + jnp.dot(high, s_low[...], preferred_element_type=F32)
        return picked, [product[:, BR * j : BR * (j + 1)] for j in range(touched)]

    def put_parts(slot, product):
        for j in range(touched):
            prod[j] = product[j]
        for k in range(2 * (2 * REACH + 1)):
            parts[slot, k] = prod[inverse[k]]

    def collect(slot, copies, coupling):
        high, low = split(coupling)
        both = lax.dot_general(
            jnp.concatenate([high, low], axis=0), one_hot[...], (((1,), (1,)), ((), ())), preferred_element_type=F32)
        spread = both[:32] + both[32:]
        for copy in copies:
            copy.wait_recv()
        result = []
        for i in range(2):
            total = parts[slot, 2 * REACH + i]
            for n in range(len(OFFSETS)):
                total = total + back[slot, n, i]
            total = total + spread[:, BR * i : BR * (i + 1)]
            result.append(total + leak[i] * halo[slot, 2 * REACH + i])
        return result

    def start_sum(slot, terms):
        stacked = jnp.concatenate(terms, axis=0)
        row = jnp.sum(stacked.T, axis=0, keepdims=True)
        group_a[slot, a_id] = row
        return [
            send(group_a.at[slot, a_id], group_a.at[slot, a_id],
                 a_send.at[slot, step - 1], a_recv.at[slot, step - 1], in_a(step))
            for step in range(1, n_a)
        ]

    def mid_sum(slot, copies):
        for copy in copies:
            copy.wait_recv()
        group_b[slot, chip] = jnp.sum(group_a[slot], axis=0)
        return [
            send(group_b.at[slot, chip], group_b.at[slot, chip],
                 b_send.at[slot, step - 1], b_recv.at[slot, step - 1], in_b(step))
            for step in range(1, n_chip)
        ]

    def end_sum(slot, copies):
        for copy in copies:
            copy.wait_recv()
        row = jnp.sum(group_b[slot], axis=0)
        return jnp.broadcast_to(row, (128, 128)).T

    halo_copies = send_halo(0)
    for i in range(6):
        loads[7 + i].wait()
        cut = pl.ds(rows * i, rows)
        high, low = split(s_full[cut])
        s_high[cut] = high
        s_low[cut] = low
    halo_copies[-1].wait_recv()
    mean_cond = 0.5 * (pad_out[0, 32:33] + pad_in[0, 32:33])
    coupling0 = mean_cond * (own_pads - pad_in[0, :32])
    for copy in halo_copies[:-1]:
        copy.wait_recv()
    picked0, product0 = apply(0)
    put_parts(0, product0)
    back_copies = send_back(0)
    curve = own_pads * coupling0
    start = jnp.zeros_like(curve)
    for j in range(touched):
        curve = curve + picked0[j] * product0[j]
    for i in range(2):
        direction = halo[0, 2 * REACH + i]
        curve = curve + leak[i] * direction * direction
        start = start + b_own[i] * direction
    sums = start_sum(0, [start, curve, jnp.zeros_like(curve), jnp.zeros_like(curve)])

    image = collect(0, back_copies, coupling0)
    for i in range(2):
        image_own[i] = image[i]
        halo[1, 2 * REACH + i] = scale[i] * image[i]
    own_pads1 = pads_of(1)
    pad_out[1, :32] = own_pads1
    halo_copies = send_halo(1)
    sums = mid_sum(0, sums)
    for copy in halo_copies:
        copy.wait_recv()
    picked1, product1 = apply(1)
    put_parts(1, product1)
    coupling1 = mean_cond * (own_pads1 - pad_in[1, :32])
    total = end_sum(0, sums)
    norm0, curve0 = total[:32], total[32:64]
    alpha0 = norm0 / curve0
    pads_z = own_pads - alpha0 * own_pads1
    curve = pads_z * (coupling0 - alpha0 * coupling1)
    for j in range(touched):
        curve = curve + (picked0[j] - alpha0 * picked1[j]) * (product0[j] - alpha0 * product1[j])
    fresh = jnp.zeros_like(curve)
    cross = jnp.zeros_like(curve)
    for i in range(2):
        residual = b_own[i] - alpha0 * image_own[i]
        z = scale[i] * residual
        fresh = fresh + residual * z
        cross = cross + z * image_own[i]
        curve = curve + leak[i] * z * z
    sums = start_sum(1, [fresh, curve, cross, jnp.zeros_like(curve)])
    back_copies = send_back(1)
    sums = mid_sum(1, sums)
    image_u = collect(1, back_copies, coupling1)
    total = end_sum(1, sums)
    norm1, zaz, zap = total[:32], total[32:64], total[64:96]
    beta = norm1 / norm0
    alpha1 = norm1 / (zaz + beta * (2.0 * zap + beta * curve0))
    for i in range(2):
        old = halo[0, 2 * REACH + i]
        residual = b_own[i] - alpha0 * image_own[i]
        direction = scale[i] * residual + beta * old
        image1 = (image_own[i] - alpha0 * image_u[i]) + beta * image_own[i]
        x_out[0, :, BR * i : BR * (i + 1)] = alpha0 * old + alpha1 * direction
        r_out[0, :, BR * i : BR * (i + 1)] = residual - alpha1 * image1
    for copy in sent:
        copy.wait_send()


def solution(mesh):
    n_board, n_sub = mesh.shape["board"], mesh.shape["sub"]
    vmem = pl.BlockSpec(memory_space=pltpu.VMEM)
    hbm = pl.BlockSpec(memory_space=pltpu.HBM)

    def on_device(rhs, schur, block_list, pad_rows, pad_cond, sink, precond):
        cases, owned = rhs.shape[1:]
        inner = schur.shape[1]
        n_off = len(OFFSETS)
        span = 2 * (2 * REACH + 1)
        dma = pltpu.SemaphoreType.DMA
        out = jax.ShapeDtypeStruct(rhs.shape, F32)
        return pl.pallas_call(
            functools.partial(kernel, n_board, n_sub),
            out_shape=(out, out),
            in_specs=[hbm] * 7,
            out_specs=(vmem, vmem),
            scratch_shapes=[
                pltpu.SMEM(block_list.shape, jnp.int32),
                pltpu.VMEM(pad_rows.shape, jnp.int32),
                pltpu.VMEM(pad_cond.shape, F32),
                pltpu.VMEM(sink.shape, F32),
                pltpu.VMEM(precond.shape, F32),
                pltpu.VMEM((2, cases, BR), F32),
                pltpu.VMEM((inner, inner), F32),
                pltpu.VMEM((inner, inner), BF16),
                pltpu.VMEM((inner, inner), BF16),
                pltpu.VMEM((owned, BR), BF16),
                pltpu.VMEM((2, cases + 8, BR), F32),
                pltpu.VMEM((2, cases + 8, BR), F32),
                pltpu.VMEM((2, span, cases, BR), F32),
                pltpu.VMEM((block_list.shape[1] + 1, cases, BR), F32),
                pltpu.VMEM((2, span, cases, BR), F32),
                pltpu.VMEM((2, n_off, 2, cases, BR), F32),
                pltpu.VMEM((2, cases, BR), F32),
                pltpu.VMEM((2, 2 * n_board, 1, 128), F32),
                pltpu.VMEM((2, n_sub // 2, 1, 128), F32),
                dma((13,)),
                dma((2, n_off)), dma((2, n_off)),
                dma((2, n_off)), dma((2, n_off)),
                dma((2,)), dma((2,)),
                dma((2, 2 * n_board - 1)), dma((2, 2 * n_board - 1)),
                dma((2, n_sub // 2 - 1)), dma((2, n_sub // 2 - 1)),
            ],
            compiler_params=pltpu.CompilerParams(
                collective_id=0, has_side_effects=True, vmem_limit_bytes=67043328
            ),
        )(rhs, schur, block_list, pad_rows, pad_cond, sink, precond)

    row = P("board", "sub")
    return jax.shard_map(
        on_device,
        mesh=mesh,
        in_specs=(P("board", None, "sub"), P("board", "sub", None), row, row, row, row, row),
        out_specs=(P("board", None, "sub"), P("board", None, "sub")),
        check_vma=False,
    )
```

```python
import functools

import jax
import jax.numpy as jnp
from jax import lax
from jax.experimental import pallas as pl
from jax.experimental.pallas import tpu as pltpu
from jax.sharding import PartitionSpec as P

BR = 128
REACH = 3
OFFSETS = (3, -3, 2, -2, 1, -1)
F32 = jnp.float32
BF16 = jnp.bfloat16


def split(value):
    high = value.astype(BF16)
    low = (value - high.astype(F32)).astype(BF16)
    return high, low


def bits(count):
    return count.bit_length() - 1


RING4 = (0, 1, 2, 1)
RING8 = (0, 1, 2, 2, 4, 3, 2, 2)


def far_first(count, hops):
    return sorted(range(1, count), key=lambda step: -hops(step))


class Copy:
    def __init__(self, copy, going, coming):
        self.copy, self.going, self.coming = copy, going, coming

    def when(self, condition, act):
        if condition is None:
            act()
        else:
            pl.when(condition)(act)

    def start(self):
        self.when(self.going, self.copy.start)

    def wait_recv(self):
        self.when(self.coming, self.copy.wait_recv)

    def wait_send(self):
        self.when(self.going, self.copy.wait_send)


def kernel(
    n_board, n_sub,
    rhs, schur, blocks_in, pad_rows_in, pad_cond_in, sink_in, precond_in,
    x_out, r_out,
    blocks, pad_rows, pad_cond, sink, precond,
    b_own, s_full, s_high, s_low, one_hot, pad_out, pad_in,
    halo, prod, parts, back, image_own, group_a, group_b,
    load_sem, halo_send, halo_recv, back_send, back_recv, pad_send, pad_recv,
    a_send, a_recv, b_send, b_recv,
):
    me_b = lax.axis_index("board")
    me_s = lax.axis_index("sub")
    core = lax.rem(me_s, 2)
    chip = lax.div(me_s, 2)
    n_a, n_chip = 2 * n_board, n_sub // 2
    a_id = me_b * 2 + core
    touched = blocks.shape[1]
    inner = schur.shape[1]
    order_a = far_first(n_a, lambda step: RING8[step // 2])
    order_b = far_first(n_chip, lambda step: RING4[step % 4] + RING8[step // 4])

    def near(offset):
        return (me_b, me_s + offset)

    def there(offset):
        if offset > 0:
            return me_s < n_sub - offset
        return me_s >= -offset

    flip_b = [(1 << k) * (1 - 2 * lax.rem(lax.div(me_b, 1 << k), 2)) for k in range(bits(n_board))]
    flip_s = [(1 << k) * (1 - 2 * lax.rem(lax.div(me_s, 1 << k), 2)) for k in range(bits(n_sub))]

    def flipped(me, flips, mask):
        for k, flip in enumerate(flips):
            if mask >> k & 1:
                me = me + flip
        return me

    def in_a(step):
        return (flipped(me_b, flip_b, step >> 1), flipped(me_s, flip_s, step & 1))

    def in_b(step):
        return (me_b, flipped(me_s, flip_s, 2 * step))

    loads = [
        pltpu.make_async_copy(rhs.at[0, :, pl.ds(BR * i, BR)], b_own.at[i], load_sem.at[i])
        for i in range(2)
    ]
    small = ((precond_in, precond), (pad_rows_in, pad_rows), (blocks_in, blocks), (pad_cond_in, pad_cond), (sink_in, sink))
    for i, (source, target) in enumerate(small):
        loads.append(pltpu.make_async_copy(source, target, load_sem.at[2 + i]))
    rows = inner // 6
    for i in range(6):
        cut = pl.ds(rows * i, rows)
        loads.append(pltpu.make_async_copy(schur.at[0, cut], s_full.at[cut], load_sem.at[7 + i]))
    for load in loads:
        load.start()

    barrier = pltpu.get_barrier_semaphore()

    def greet(device):
        pl.semaphore_signal(barrier, inc=1, device_id=device, device_id_type=pl.DeviceIdType.MESH)

    beside = 2 * core - 1
    inside = jnp.logical_and(me_s + beside >= 0, me_s + beside < n_sub)
    for offset in (3, -3):
        pl.when(there(offset))(lambda: greet(near(offset)))
    pl.when(inside)(lambda: greet((me_b, me_s + beside)))
    for step in order_b:
        greet(in_b(step))
    for step in order_a:
        greet(in_a(step))

    for load in loads[:3]:
        load.wait()
    scale = [precond[0:1, BR * i : BR * (i + 1)] for i in range(2)]
    for i in range(2):
        halo[0, 2 * REACH + i] = scale[i] * b_own[i]
    count = inside.astype(jnp.int32) + there(3).astype(jnp.int32) + there(-3).astype(jnp.int32)
    pl.semaphore_wait(barrier, count + n_a - 1 + n_chip - 1)

    sent = []

    def send(source, target, send_sem, recv_sem, device, going=None, coming=None):
        copy = Copy(pltpu.make_async_remote_copy(
            src_ref=source, dst_ref=target, send_sem=send_sem, recv_sem=recv_sem,
            device_id=device, device_id_type=pl.DeviceIdType.MESH,
        ), going, coming)
        copy.start()
        sent.append(copy)
        return copy

    def send_halo(slot):
        copies = []
        for n, offset in enumerate(OFFSETS):
            copies.append(send(
                halo.at[slot, pl.ds(2 * REACH, 2)], halo.at[slot, pl.ds(2 * (REACH - offset), 2)],
                halo_send.at[slot, n], halo_recv.at[slot, n], near(offset), there(offset), there(-offset)))
        return copies

    def send_pads(slot):
        return send(pad_out.at[slot], pad_in.at[slot], pad_send.at[slot], pad_recv.at[slot], in_a(2))

    def pads_of(slot):
        high, low = split(jnp.concatenate([halo[slot, 2 * REACH], halo[slot, 2 * REACH + 1]], axis=1))
        both = jnp.dot(jnp.concatenate([high, low], axis=0), one_hot[...], preferred_element_type=F32)
        return both[:32] + both[32:]

    def send_back(slot):
        copies = []
        for n, offset in enumerate(OFFSETS):
            copies.append(send(
                parts.at[slot, pl.ds(2 * (REACH + offset), 2)], back.at[slot, n],
                back_send.at[slot, n], back_recv.at[slot, n], near(offset), there(offset), there(-offset)))
        return copies

    def apply(slot):
        picked = [halo[slot, index[j]] for j in range(touched)]
        splits = [split(block) for block in picked]
        high = jnp.concatenate([pair[0] for pair in splits], axis=1)
        low = jnp.concatenate([pair[1] for pair in splits], axis=1)
        both = jnp.dot(jnp.concatenate([high, low], axis=0), s_high[...], preferred_element_type=F32)
        product = both[:32] + both[32:] + jnp.dot(high, s_low[...], preferred_element_type=F32)
        return picked, [product[:, BR * j : BR * (j + 1)] for j in range(touched)]

    def put_parts(slot, product):
        for j in range(touched):
            prod[j] = product[j]
        for k in range(2 * (2 * REACH + 1)):
            parts[slot, k] = prod[inverse[k]]

    def collect(slot, copies, coupling):
        high, low = split(coupling)
        both = lax.dot_general(
            jnp.concatenate([high, low], axis=0), one_hot[...], (((1,), (1,)), ((), ())), preferred_element_type=F32)
        spread = both[:32] + both[32:]
        for copy in copies:
            copy.wait_recv()
        result = []
        for i in range(2):
            total = parts[slot, 2 * REACH + i]
            for n in range(len(OFFSETS)):
                total = total + back[slot, n, i]
            total = total + spread[:, BR * i : BR * (i + 1)]
            result.append(total + leak[i] * halo[slot, 2 * REACH + i])
        return result

    halo_copies = send_halo(0)
    for load in loads[3:7]:
        load.wait()
    leak = [sink[0:1, BR * i : BR * (i + 1)] for i in range(2)]
    n_pads = pad_rows.shape[1]
    row_ids = lax.broadcasted_iota(jnp.int32, (2 * BR, n_pads), 0)
    one_hot[...] = jnp.zeros_like(one_hot)
    one_hot[:, :n_pads] = jnp.where(row_ids == pad_rows[...], 1.0, 0.0).astype(BF16)
    own_pads = pads_of(0)
    pad_out[...] = jnp.zeros_like(pad_out)
    pad_out[0, :32] = own_pads
    pad_out[0, 32:33, :n_pads] = pad_cond[...]
    pads_copy = send_pads(0)
    last = 2 * (2 * REACH + 1) - 1
    index = [jnp.clip(blocks[0, j] - (me_s - REACH) * 2, 0, last) for j in range(touched)]
    inverse = []
    for k in range(last + 1):
        where = jnp.int32(touched)
        for j in range(touched):
            where = jnp.where(index[j] == k, j, where)
        inverse.append(where)
    prod[touched] = jnp.zeros_like(prod[touched])

    for n, offset in enumerate(OFFSETS):
        @pl.when(jnp.logical_not(there(-offset)))
        def _():
            for slot in range(2):
                back[slot, n] = jnp.zeros_like(back[slot, n])
                halo[slot, 2 * (REACH - offset) : 2 * (REACH - offset) + 2] = jnp.zeros((2, 32, BR), F32)

    for i in range(6):
        loads[7 + i].wait()
        cut = pl.ds(rows * i, rows)
        high, low = split(s_full[cut])
        s_high[cut] = high
        s_low[cut] = low
    for copy in halo_copies:
        copy.wait_recv()
    picked, product = apply(0)
    put_parts(0, product)
    back_copies = send_back(0)
    pads_copy.wait_recv()
    mean_cond = 0.5 * (pad_out[0, 32:33] + pad_in[0, 32:33])
    image = collect(0, back_copies, mean_cond * (own_pads - pad_in[0, :32]))

    for i in range(2):
        image_own[i] = image[i]
        halo[1, 2 * REACH + i] = scale[i] * image[i]
    halo_copies = send_halo(1)
    own_pads = pads_of(1)
    pad_out[1, :32] = own_pads
    pads_copy = send_pads(1)
    moments = [jnp.zeros((32, BR), F32)] * 4
    for i in range(2):
        old, u = halo[0, 2 * REACH + i], halo[1, 2 * REACH + i]
        moments = [
            moments[0] + b_own[i] * old,
            moments[1] + old * image[i],
            moments[2] + u * image[i],
            moments[3] + leak[i] * u * u,
        ]
    pads_copy.wait_recv()
    coupling = mean_cond * (own_pads - pad_in[1, :32])
    moments[3] = moments[3] + own_pads * coupling
    for copy in halo_copies:
        copy.wait_recv()
    picked, product = apply(1)
    for j in range(touched):
        moments[3] = moments[3] + picked[j] * product[j]

    group_a[a_id] = jnp.sum(jnp.concatenate(moments, axis=0).T, axis=0, keepdims=True)
    copies = [
        send(group_a.at[a_id], group_a.at[a_id], a_send.at[step - 1], a_recv.at[step - 1], in_a(step))
        for step in order_a
    ]
    put_parts(1, product)
    back_copies = send_back(1)
    for copy in copies:
        copy.wait_recv()
    group_b[chip] = jnp.sum(group_a[...], axis=0)
    copies = [
        send(group_b.at[chip], group_b.at[chip], b_send.at[step - 1], b_recv.at[step - 1], in_b(step))
        for step in order_b
    ]
    image_u = collect(1, back_copies, coupling)
    for copy in copies:
        copy.wait_recv()
    total = jnp.broadcast_to(jnp.sum(group_b[...], axis=0), (128, 128)).T
    m0, m1, m2, m3 = [total[32 * k : 32 * (k + 1)] for k in range(4)]
    alpha0 = m0 / m1
    cross = m1 - alpha0 * m2
    fresh = (m0 - alpha0 * m1) - alpha0 * cross
    beta = fresh / m0
    bend = cross - alpha0 * (m2 - alpha0 * m3)
    alpha1 = fresh / (bend + beta * (2.0 * cross + beta * m1))
    for i in range(2):
        old = halo[0, 2 * REACH + i]
        residual = b_own[i] - alpha0 * image_own[i]
        direction = scale[i] * residual + beta * old
        image1 = (image_own[i] - alpha0 * image_u[i]) + beta * image_own[i]
        x_out[0, :, BR * i : BR * (i + 1)] = alpha0 * old + alpha1 * direction
        r_out[0, :, BR * i : BR * (i + 1)] = residual - alpha1 * image1
    for copy in sent:
        copy.wait_send()


def put_out(x_in, r_in, x_out, r_out, sem):
    copies = [
        pltpu.make_async_copy(x_in, x_out, sem.at[0]),
        pltpu.make_async_copy(r_in, r_out, sem.at[1]),
    ]
    for copy in copies:
        copy.start()
    for copy in copies:
        copy.wait()


def solution(mesh):
    n_board, n_sub = mesh.shape["board"], mesh.shape["sub"]
    vmem = pl.BlockSpec(memory_space=pltpu.VMEM)
    hbm = pl.BlockSpec(memory_space=pltpu.HBM)

    def on_device(rhs, schur, block_list, pad_rows, pad_cond, sink, precond):
        cases, owned = rhs.shape[1:]
        inner = schur.shape[1]
        n_off = len(OFFSETS)
        span = 2 * (2 * REACH + 1)
        dma = pltpu.SemaphoreType.DMA
        out = jax.ShapeDtypeStruct(rhs.shape, F32)
        results = pl.pallas_call(
            functools.partial(kernel, n_board, n_sub),
            out_shape=(out, out),
            in_specs=[hbm] * 7,
            out_specs=(vmem, vmem),
            scratch_shapes=[
                pltpu.SMEM(block_list.shape, jnp.int32),
                pltpu.VMEM(pad_rows.shape, jnp.int32),
                pltpu.VMEM(pad_cond.shape, F32),
                pltpu.VMEM(sink.shape, F32),
                pltpu.VMEM(precond.shape, F32),
                pltpu.VMEM((2, cases, BR), F32),
                pltpu.VMEM((inner, inner), F32),
                pltpu.VMEM((inner, inner), BF16),
                pltpu.VMEM((inner, inner), BF16),
                pltpu.VMEM((owned, BR), BF16),
                pltpu.VMEM((2, cases + 8, BR), F32),
                pltpu.VMEM((2, cases + 8, BR), F32),
                pltpu.VMEM((2, span, cases, BR), F32),
                pltpu.VMEM((block_list.shape[1] + 1, cases, BR), F32),
                pltpu.VMEM((2, span, cases, BR), F32),
                pltpu.VMEM((2, n_off, 2, cases, BR), F32),
                pltpu.VMEM((2, cases, BR), F32),
                pltpu.VMEM((2 * n_board, 1, 128), F32),
                pltpu.VMEM((n_sub // 2, 1, 128), F32),
                dma((13,)),
                dma((2, n_off)), dma((2, n_off)),
                dma((2, n_off)), dma((2, n_off)),
                dma((2,)), dma((2,)),
                dma((2 * n_board - 1,)), dma((2 * n_board - 1,)),
                dma((n_sub // 2 - 1,)), dma((n_sub // 2 - 1,)),
            ],
            compiler_params=pltpu.CompilerParams(
                collective_id=0, has_side_effects=True, vmem_limit_bytes=32 * 1024 * 1024
            ),
        )(*[pltpu.with_memory_space_constraint(a, pltpu.HBM) for a in (rhs, schur, block_list, pad_rows, pad_cond, sink, precond)])
        return pl.pallas_call(
            put_out,
            out_shape=(out, out),
            in_specs=[vmem, vmem],
            out_specs=(hbm, hbm),
            scratch_shapes=[dma((2,))],
            compiler_params=pltpu.CompilerParams(vmem_limit_bytes=8 * 1024 * 1024),
        )(*results)

    row = P("board", "sub")
    return jax.shard_map(
        on_device,
        mesh=mesh,
        in_specs=(P("board", None, "sub"), P("board", "sub", None), row, row, row, row, row),
        out_specs=(P("board", None, "sub"), P("board", None, "sub")),
        check_vma=False,
    )
```

```python
import functools

import jax
import jax.numpy as jnp
from jax import lax
from jax.experimental import pallas as pl
from jax.experimental.pallas import tpu as pltpu
from jax.sharding import PartitionSpec as P

BR = 128
REACH = 3
OFFSETS = (3, -3, 2, -2, 1, -1)
F32 = jnp.float32
BF16 = jnp.bfloat16


def split(value):
    high = value.astype(BF16)
    low = (value - high.astype(F32)).astype(BF16)
    return high, low


def bits(count):
    return count.bit_length() - 1


RING4 = (0, 1, 2, 1)
RING8 = (0, 1, 2, 2, 4, 3, 2, 2)


def far_first(count, hops):
    return sorted(range(1, count), key=lambda step: -hops(step))


class Copy:
    def __init__(self, copy, going, coming):
        self.copy, self.going, self.coming = copy, going, coming

    def when(self, condition, act):
        if condition is None:
            act()
        else:
            pl.when(condition)(act)

    def start(self):
        self.when(self.going, self.copy.start)

    def wait_recv(self):
        self.when(self.coming, self.copy.wait_recv)

    def wait_send(self):
        self.when(self.going, self.copy.wait_send)


def kernel(
    n_board, n_sub,
    rhs, schur, blocks_in, pad_rows_in, pad_cond_in, sink_in, precond_in,
    x_out, r_out,
    blocks, pad_rows, pad_cond, sink, precond,
    b_own, s_full, s_high, s_low, one_hot, pad_out, pad_in,
    halo, prod, parts, back, image_own, group_a, group_b,
    load_sem, halo_send, halo_recv, back_send, back_recv, pad_send, pad_recv,
    a_send, a_recv, b_send, b_recv, relay,
):
    me_b = lax.axis_index("board")
    me_s = lax.axis_index("sub")
    core = lax.rem(me_s, 2)
    chip = lax.div(me_s, 2)
    n_a, n_chip = 2 * n_board, n_sub // 2
    a_id = me_b * 2 + core
    touched = blocks.shape[1]
    inner = schur.shape[1]
    order_a = far_first(n_a, lambda step: RING8[step // 2])
    order_b = far_first(n_chip, lambda step: RING4[step % 4] + RING8[step // 4])

    def near(offset):
        return (me_b, me_s + offset)

    def there(offset):
        if offset > 0:
            return me_s < n_sub - offset
        return me_s >= -offset

    flip_b = [(1 << k) * (1 - 2 * lax.rem(lax.div(me_b, 1 << k), 2)) for k in range(bits(n_board))]
    flip_s = [(1 << k) * (1 - 2 * lax.rem(lax.div(me_s, 1 << k), 2)) for k in range(bits(n_sub))]

    def flipped(me, flips, mask):
        for k, flip in enumerate(flips):
            if mask >> k & 1:
                me = me + flip
        return me

    def in_a(step):
        return (flipped(me_b, flip_b, step >> 1), flipped(me_s, flip_s, step & 1))

    def in_b(step):
        return (me_b, flipped(me_s, flip_s, 2 * step))

    def steps(count):
        return sorted({step % count for step in (1, -1, 2, -2)} - {0})

    layer = 8
    ring_b = [(lax.rem(me_b + step, n_board), me_s) for step in steps(n_board)]
    ring_s = [(me_b, lax.rem(me_s + layer * step, n_sub)) for step in steps(n_sub // layer)]
    row = [in_b(step) for step in range(1, layer // 2)]

    loads = [
        pltpu.make_async_copy(rhs.at[0, :, pl.ds(BR * i, BR)], b_own.at[i], load_sem.at[i])
        for i in range(2)
    ]
    small = ((precond_in, precond), (pad_rows_in, pad_rows), (blocks_in, blocks), (pad_cond_in, pad_cond), (sink_in, sink))
    for i, (source, target) in enumerate(small):
        loads.append(pltpu.make_async_copy(source, target, load_sem.at[2 + i]))
    rows = inner // 6
    for i in range(6):
        cut = pl.ds(rows * i, rows)
        loads.append(pltpu.make_async_copy(schur.at[0, cut], s_full.at[cut], load_sem.at[7 + i]))
    for load in loads:
        load.start()

    barrier = pltpu.get_barrier_semaphore()

    def greet(device):
        pl.semaphore_signal(barrier, inc=1, device_id=device, device_id_type=pl.DeviceIdType.MESH)

    count = len(ring_b) + len(ring_s) + len(row)
    for offset in OFFSETS:
        pl.when(there(offset))(lambda: greet(near(offset)))
        count = count + there(offset).astype(jnp.int32)
    for device in row + ring_b + ring_s:
        greet(device)

    for load in loads[:3]:
        load.wait()
    scale = [precond[0:1, BR * i : BR * (i + 1)] for i in range(2)]
    for i in range(2):
        halo[0, 2 * REACH + i] = scale[i] * b_own[i]
    pl.semaphore_wait(barrier, count)

    def pass_on(turn):
        for device in ring_b + ring_s:
            pl.semaphore_signal(relay.at[turn], inc=1, device_id=device, device_id_type=pl.DeviceIdType.MESH)

    def hear(turn):
        pl.semaphore_wait(relay.at[turn], len(ring_b) + len(ring_s))

    sent = []

    def send(source, target, send_sem, recv_sem, device, going=None, coming=None):
        copy = Copy(pltpu.make_async_remote_copy(
            src_ref=source, dst_ref=target, send_sem=send_sem, recv_sem=recv_sem,
            device_id=device, device_id_type=pl.DeviceIdType.MESH,
        ), going, coming)
        copy.start()
        sent.append(copy)
        return copy

    def send_halo(slot):
        copies = []
        for n, offset in enumerate(OFFSETS):
            copies.append(send(
                halo.at[slot, pl.ds(2 * REACH, 2)], halo.at[slot, pl.ds(2 * (REACH - offset), 2)],
                halo_send.at[slot, n], halo_recv.at[slot, n], near(offset), there(offset), there(-offset)))
        return copies

    def send_pads(slot):
        return send(pad_out.at[slot], pad_in.at[slot], pad_send.at[slot], pad_recv.at[slot], in_a(2))

    def pads_of(slot):
        high, low = split(jnp.concatenate([halo[slot, 2 * REACH], halo[slot, 2 * REACH + 1]], axis=1))
        both = jnp.dot(jnp.concatenate([high, low], axis=0), one_hot[...], preferred_element_type=F32)
        return both[:32] + both[32:]

    def send_back(slot):
        copies = []
        for n, offset in enumerate(OFFSETS):
            copies.append(send(
                parts.at[slot, pl.ds(2 * (REACH + offset), 2)], back.at[slot, n],
                back_send.at[slot, n], back_recv.at[slot, n], near(offset), there(offset), there(-offset)))
        return copies

    def apply(slot):
        picked = [halo[slot, index[j]] for j in range(touched)]
        splits = [split(block) for block in picked]
        high = jnp.concatenate([pair[0] for pair in splits], axis=1)
        low = jnp.concatenate([pair[1] for pair in splits], axis=1)
        both = jnp.dot(jnp.concatenate([high, low], axis=0), s_high[...], preferred_element_type=F32)
        product = both[:32] + both[32:] + jnp.dot(high, s_low[...], preferred_element_type=F32)
        return picked, [product[:, BR * j : BR * (j + 1)] for j in range(touched)]

    def put_parts(slot, product):
        for j in range(touched):
            prod[j] = product[j]
        for k in range(2 * (2 * REACH + 1)):
            parts[slot, k] = prod[inverse[k]]

    def collect(slot, copies, coupling):
        high, low = split(coupling)
        both = lax.dot_general(
            jnp.concatenate([high, low], axis=0), one_hot[...], (((1,), (1,)), ((), ())), preferred_element_type=F32)
        spread = both[:32] + both[32:]
        for copy in copies:
            copy.wait_recv()
        result = []
        for i in range(2):
            total = parts[slot, 2 * REACH + i]
            for n in range(len(OFFSETS)):
                total = total + back[slot, n, i]
            total = total + spread[:, BR * i : BR * (i + 1)]
            result.append(total + leak[i] * halo[slot, 2 * REACH + i])
        return result

    halo_copies = send_halo(0)
    pass_on(0)
    for load in loads[3:7]:
        load.wait()
    leak = [sink[0:1, BR * i : BR * (i + 1)] for i in range(2)]
    n_pads = pad_rows.shape[1]
    row_ids = lax.broadcasted_iota(jnp.int32, (2 * BR, n_pads), 0)
    one_hot[...] = jnp.zeros_like(one_hot)
    one_hot[:, :n_pads] = jnp.where(row_ids == pad_rows[...], 1.0, 0.0).astype(BF16)
    own_pads = pads_of(0)
    pad_out[...] = jnp.zeros_like(pad_out)
    pad_out[0, :32] = own_pads
    pad_out[0, 32:33, :n_pads] = pad_cond[...]
    pads_copy = send_pads(0)
    last = 2 * (2 * REACH + 1) - 1
    index = [jnp.clip(blocks[0, j] - (me_s - REACH) * 2, 0, last) for j in range(touched)]
    inverse = []
    for k in range(last + 1):
        where = jnp.int32(touched)
        for j in range(touched):
            where = jnp.where(index[j] == k, j, where)
        inverse.append(where)
    prod[touched] = jnp.zeros_like(prod[touched])

    for n, offset in enumerate(OFFSETS):
        @pl.when(jnp.logical_not(there(-offset)))
        def _():
            for slot in range(2):
                back[slot, n] = jnp.zeros_like(back[slot, n])
                halo[slot, 2 * (REACH - offset) : 2 * (REACH - offset) + 2] = jnp.zeros((2, 32, BR), F32)

    for i in range(6):
        loads[7 + i].wait()
        cut = pl.ds(rows * i, rows)
        high, low = split(s_full[cut])
        s_high[cut] = high
        s_low[cut] = low
    for copy in halo_copies:
        copy.wait_recv()
    picked, product = apply(0)
    put_parts(0, product)
    back_copies = send_back(0)
    hear(0)
    pass_on(1)
    pads_copy.wait_recv()
    mean_cond = 0.5 * (pad_out[0, 32:33] + pad_in[0, 32:33])
    image = collect(0, back_copies, mean_cond * (own_pads - pad_in[0, :32]))

    for i in range(2):
        image_own[i] = image[i]
        halo[1, 2 * REACH + i] = scale[i] * image[i]
    halo_copies = send_halo(1)
    own_pads = pads_of(1)
    pad_out[1, :32] = own_pads
    pads_copy = send_pads(1)
    moments = [jnp.zeros((32, BR), F32)] * 4
    for i in range(2):
        old, u = halo[0, 2 * REACH + i], halo[1, 2 * REACH + i]
        moments = [
            moments[0] + b_own[i] * old,
            moments[1] + old * image[i],
            moments[2] + u * image[i],
            moments[3] + leak[i] * u * u,
        ]
    pads_copy.wait_recv()
    coupling = mean_cond * (own_pads - pad_in[1, :32])
    moments[3] = moments[3] + own_pads * coupling
    for copy in halo_copies:
        copy.wait_recv()
    picked, product = apply(1)
    for j in range(touched):
        moments[3] = moments[3] + picked[j] * product[j]

    hear(1)

    group_a[a_id] = jnp.sum(jnp.concatenate(moments, axis=0).T, axis=0, keepdims=True)
    copies = [
        send(group_a.at[a_id], group_a.at[a_id], a_send.at[step - 1], a_recv.at[step - 1], in_a(step))
        for step in order_a
    ]
    put_parts(1, product)
    back_copies = send_back(1)
    for copy in copies:
        copy.wait_recv()
    group_b[chip] = jnp.sum(group_a[...], axis=0)
    copies = [
        send(group_b.at[chip], group_b.at[chip], b_send.at[step - 1], b_recv.at[step - 1], in_b(step))
        for step in order_b
    ]
    image_u = collect(1, back_copies, coupling)
    for copy in copies:
        copy.wait_recv()
    total = jnp.broadcast_to(jnp.sum(group_b[...], axis=0), (128, 128)).T
    m0, m1, m2, m3 = [total[32 * k : 32 * (k + 1)] for k in range(4)]
    alpha0 = m0 / m1
    cross = m1 - alpha0 * m2
    fresh = (m0 - alpha0 * m1) - alpha0 * cross
    beta = fresh / m0
    bend = cross - alpha0 * (m2 - alpha0 * m3)
    alpha1 = fresh / (bend + beta * (2.0 * cross + beta * m1))
    for i in range(2):
        old = halo[0, 2 * REACH + i]
        residual = b_own[i] - alpha0 * image_own[i]
        direction = scale[i] * residual + beta * old
        image1 = (image_own[i] - alpha0 * image_u[i]) + beta * image_own[i]
        x_out[0, :, BR * i : BR * (i + 1)] = alpha0 * old + alpha1 * direction
        r_out[0, :, BR * i : BR * (i + 1)] = residual - alpha1 * image1
    for copy in sent:
        copy.wait_send()


def put_out(x_in, r_in, x_out, r_out, sem):
    copies = [
        pltpu.make_async_copy(x_in, x_out, sem.at[0]),
        pltpu.make_async_copy(r_in, r_out, sem.at[1]),
    ]
    for copy in copies:
        copy.start()
    for copy in copies:
        copy.wait()


def solution(mesh):
    n_board, n_sub = mesh.shape["board"], mesh.shape["sub"]
    vmem = pl.BlockSpec(memory_space=pltpu.VMEM)
    hbm = pl.BlockSpec(memory_space=pltpu.HBM)

    def on_device(rhs, schur, block_list, pad_rows, pad_cond, sink, precond):
        cases, owned = rhs.shape[1:]
        inner = schur.shape[1]
        n_off = len(OFFSETS)
        span = 2 * (2 * REACH + 1)
        dma = pltpu.SemaphoreType.DMA
        out = jax.ShapeDtypeStruct(rhs.shape, F32)
        results = pl.pallas_call(
            functools.partial(kernel, n_board, n_sub),
            out_shape=(out, out),
            in_specs=[hbm] * 7,
            out_specs=(vmem, vmem),
            scratch_shapes=[
                pltpu.SMEM(block_list.shape, jnp.int32),
                pltpu.VMEM(pad_rows.shape, jnp.int32),
                pltpu.VMEM(pad_cond.shape, F32),
                pltpu.VMEM(sink.shape, F32),
                pltpu.VMEM(precond.shape, F32),
                pltpu.VMEM((2, cases, BR), F32),
                pltpu.VMEM((inner, inner), F32),
                pltpu.VMEM((inner, inner), BF16),
                pltpu.VMEM((inner, inner), BF16),
                pltpu.VMEM((owned, BR), BF16),
                pltpu.VMEM((2, cases + 8, BR), F32),
                pltpu.VMEM((2, cases + 8, BR), F32),
                pltpu.VMEM((2, span, cases, BR), F32),
                pltpu.VMEM((block_list.shape[1] + 1, cases, BR), F32),
                pltpu.VMEM((2, span, cases, BR), F32),
                pltpu.VMEM((2, n_off, 2, cases, BR), F32),
                pltpu.VMEM((2, cases, BR), F32),
                pltpu.VMEM((2 * n_board, 1, 128), F32),
                pltpu.VMEM((n_sub // 2, 1, 128), F32),
                dma((13,)),
                dma((2, n_off)), dma((2, n_off)),
                dma((2, n_off)), dma((2, n_off)),
                dma((2,)), dma((2,)),
                dma((2 * n_board - 1,)), dma((2 * n_board - 1,)),
                dma((n_sub // 2 - 1,)), dma((n_sub // 2 - 1,)),
                pltpu.SemaphoreType.REGULAR((2,)),
            ],
            compiler_params=pltpu.CompilerParams(
                collective_id=0, has_side_effects=True, vmem_limit_bytes=32 * 1024 * 1024
            ),
        )(*[pltpu.with_memory_space_constraint(a, pltpu.HBM) for a in (rhs, schur, block_list, pad_rows, pad_cond, sink, precond)])
        return pl.pallas_call(
            put_out,
            out_shape=(out, out),
            in_specs=[vmem, vmem],
            out_specs=(hbm, hbm),
            scratch_shapes=[dma((2,))],
            compiler_params=pltpu.CompilerParams(vmem_limit_bytes=8 * 1024 * 1024),
        )(*results)

    row = P("board", "sub")
    return jax.shard_map(
        on_device,
        mesh=mesh,
        in_specs=(P("board", None, "sub"), P("board", "sub", None), row, row, row, row, row),
        out_specs=(P("board", None, "sub"), P("board", None, "sub")),
        check_vma=False,
    )
```

```python
import functools

import jax
import jax.numpy as jnp
from jax import lax
from jax.experimental import pallas as pl
from jax.experimental.pallas import tpu as pltpu
from jax.sharding import PartitionSpec as P

BR = 128
REACH = 3
OFFSETS = (3, -3, 2, -2, 1, -1)
F32 = jnp.float32
BF16 = jnp.bfloat16


def split(value):
    high = value.astype(BF16)
    low = (value - high.astype(F32)).astype(BF16)
    return high, low


def bits(count):
    return count.bit_length() - 1


RING4 = (0, 1, 2, 1)
RING8 = (0, 1, 2, 2, 4, 3, 2, 2)


def far_first(count, hops):
    return sorted(range(1, count), key=lambda step: -hops(step))


class Copy:
    def __init__(self, copy, going, coming):
        self.copy, self.going, self.coming = copy, going, coming

    def when(self, condition, act):
        if condition is None:
            act()
        else:
            pl.when(condition)(act)

    def start(self):
        self.when(self.going, self.copy.start)

    def wait_recv(self):
        self.when(self.coming, self.copy.wait_recv)

    def wait_send(self):
        self.when(self.going, self.copy.wait_send)


def kernel(
    n_board, n_sub,
    rhs, schur, blocks_in, pad_rows_in, pad_cond_in, sink_in, precond_in,
    x_out, r_out,
    blocks, pad_rows, pad_cond, sink, precond,
    b_own, s_full, s_high, s_low, one_hot, pad_out, pad_in,
    halo, prod, parts, back, image_own, group_a, group_b,
    load_sem, halo_send, halo_recv, back_send, back_recv, pad_send, pad_recv,
    a_send, a_recv, b_send, b_recv, relay,
):
    me_b = lax.axis_index("board")
    me_s = lax.axis_index("sub")
    core = lax.rem(me_s, 2)
    chip = lax.div(me_s, 2)
    n_a, n_chip = 2 * n_board, n_sub // 2
    a_id = me_b * 2 + core
    touched = blocks.shape[1]
    inner = schur.shape[1]
    order_a = far_first(n_a, lambda step: RING8[step // 2])
    order_b = far_first(n_chip, lambda step: RING4[step % 4] + RING8[step // 4])

    def near(offset):
        return (me_b, me_s + offset)

    def there(offset):
        if offset > 0:
            return me_s < n_sub - offset
        return me_s >= -offset

    flip_b = [(1 << k) * (1 - 2 * lax.rem(lax.div(me_b, 1 << k), 2)) for k in range(bits(n_board))]
    flip_s = [(1 << k) * (1 - 2 * lax.rem(lax.div(me_s, 1 << k), 2)) for k in range(bits(n_sub))]

    def flipped(me, flips, mask):
        for k, flip in enumerate(flips):
            if mask >> k & 1:
                me = me + flip
        return me

    def in_a(step):
        return (flipped(me_b, flip_b, step >> 1), flipped(me_s, flip_s, step & 1))

    def in_b(step):
        return (me_b, flipped(me_s, flip_s, 2 * step))

    def steps(count):
        return sorted({step % count for step in (1, -1, 2, -2)} - {0})

    layer = 8
    ring_b = [(lax.rem(me_b + step, n_board), me_s) for step in steps(n_board)]
    ring_s = [(me_b, lax.rem(me_s + layer * step, n_sub)) for step in steps(n_sub // layer)]
    row = [in_b(step) for step in range(1, layer // 2)]

    barrier = pltpu.get_barrier_semaphore()

    def greet(device):
        pl.semaphore_signal(barrier, inc=1, device_id=device, device_id_type=pl.DeviceIdType.MESH)

    count = len(ring_b) + len(ring_s) + len(row)
    for offset in OFFSETS:
        pl.when(there(offset))(lambda: greet(near(offset)))
        count = count + there(offset).astype(jnp.int32)
    for device in row + ring_b + ring_s:
        greet(device)

    loads = [
        pltpu.make_async_copy(rhs.at[0, :, pl.ds(BR * i, BR)], b_own.at[i], load_sem.at[i])
        for i in range(2)
    ]
    small = ((precond_in, precond), (pad_rows_in, pad_rows), (blocks_in, blocks), (pad_cond_in, pad_cond), (sink_in, sink))
    for i, (source, target) in enumerate(small):
        loads.append(pltpu.make_async_copy(source, target, load_sem.at[2 + i]))
    rows = inner // 6
    for i in range(6):
        cut = pl.ds(rows * i, rows)
        loads.append(pltpu.make_async_copy(schur.at[0, cut], s_full.at[cut], load_sem.at[7 + i]))
    for load in loads:
        load.start()

    for load in loads[:3]:
        load.wait()
    scale = [precond[0:1, BR * i : BR * (i + 1)] for i in range(2)]
    for i in range(2):
        halo[0, 2 * REACH + i] = scale[i] * b_own[i]
    pl.semaphore_wait(barrier, count)

    def pass_on(turn):
        for device in ring_b + ring_s:
            pl.semaphore_signal(relay.at[turn], inc=1, device_id=device, device_id_type=pl.DeviceIdType.MESH)

    def hear(turn):
        pl.semaphore_wait(relay.at[turn], len(ring_b) + len(ring_s))

    sent = []

    def send(source, target, send_sem, recv_sem, device, going=None, coming=None):
        copy = Copy(pltpu.make_async_remote_copy(
            src_ref=source, dst_ref=target, send_sem=send_sem, recv_sem=recv_sem,
            device_id=device, device_id_type=pl.DeviceIdType.MESH,
        ), going, coming)
        copy.start()
        sent.append(copy)
        return copy

    def spread_row(group, me, send_sem, recv_sem, devices):
        for device in devices:
            pltpu.make_async_remote_copy(
                src_ref=group.at[me], dst_ref=group.at[me], send_sem=send_sem, recv_sem=recv_sem,
                device_id=device, device_id_type=pl.DeviceIdType.MESH,
            ).start()
        others = group.at[pl.ds(0, len(devices))]
        return pltpu.make_async_remote_copy(
            src_ref=others, dst_ref=others, send_sem=send_sem, recv_sem=recv_sem,
            device_id=devices[0], device_id_type=pl.DeviceIdType.MESH,
        )

    def send_halo(slot):
        copies = []
        for n, offset in enumerate(OFFSETS):
            copies.append(send(
                halo.at[slot, pl.ds(2 * REACH, 2)], halo.at[slot, pl.ds(2 * (REACH - offset), 2)],
                halo_send.at[slot, n], halo_recv.at[slot, n], near(offset), there(offset), there(-offset)))
        return copies

    def send_pads(slot):
        return send(pad_out.at[slot], pad_in.at[slot], pad_send.at[slot], pad_recv.at[slot], in_a(2))

    def pads_of(slot):
        high, low = split(jnp.concatenate([halo[slot, 2 * REACH], halo[slot, 2 * REACH + 1]], axis=1))
        both = jnp.dot(jnp.concatenate([high, low], axis=0), one_hot[...], preferred_element_type=F32)
        return both[:32] + both[32:]

    def send_back(slot):
        copies = []
        for n, offset in enumerate(OFFSETS):
            copies.append(send(
                parts.at[slot, pl.ds(2 * (REACH + offset), 2)], back.at[slot, n],
                back_send.at[slot, n], back_recv.at[slot, n], near(offset), there(offset), there(-offset)))
        return copies

    def apply(slot):
        picked = [halo[slot, index[j]] for j in range(touched)]
        splits = [split(block) for block in picked]
        high = jnp.concatenate([pair[0] for pair in splits], axis=1)
        low = jnp.concatenate([pair[1] for pair in splits], axis=1)
        both = jnp.dot(jnp.concatenate([high, low], axis=0), s_high[...], preferred_element_type=F32)
        product = both[:32] + both[32:] + jnp.dot(high, s_low[...], preferred_element_type=F32)
        return picked, [product[:, BR * j : BR * (j + 1)] for j in range(touched)]

    def put_parts(slot, product):
        for j in range(touched):
            prod[j] = product[j]
        for k in range(2 * (2 * REACH + 1)):
            parts[slot, k] = prod[inverse[k]]

    def collect(slot, copies, coupling):
        high, low = split(coupling)
        both = lax.dot_general(
            jnp.concatenate([high, low], axis=0), one_hot[...], (((1,), (1,)), ((), ())), preferred_element_type=F32)
        spread = both[:32] + both[32:]
        for copy in copies:
            copy.wait_recv()
        result = []
        for i in range(2):
            total = parts[slot, 2 * REACH + i]
            for n in range(len(OFFSETS)):
                total = total + back[slot, n, i]
            total = total + spread[:, BR * i : BR * (i + 1)]
            result.append(total + leak[i] * halo[slot, 2 * REACH + i])
        return result

    halo_copies = send_halo(0)
    pass_on(0)
    for load in loads[3:7]:
        load.wait()
    leak = [sink[0:1, BR * i : BR * (i + 1)] for i in range(2)]
    n_pads = pad_rows.shape[1]
    row_ids = lax.broadcasted_iota(jnp.int32, (2 * BR, n_pads), 0)
    one_hot[...] = jnp.zeros_like(one_hot)
    one_hot[:, :n_pads] = jnp.where(row_ids == pad_rows[...], 1.0, 0.0).astype(BF16)
    own_pads = pads_of(0)
    pad_out[...] = jnp.zeros_like(pad_out)
    pad_out[0, :32] = own_pads
    pad_out[0, 32:33, :n_pads] = pad_cond[...]
    pads_copy = send_pads(0)
    last = 2 * (2 * REACH + 1) - 1
    index = [jnp.clip(blocks[0, j] - (me_s - REACH) * 2, 0, last) for j in range(touched)]
    inverse = []
    for k in range(last + 1):
        where = jnp.int32(touched)
        for j in range(touched):
            where = jnp.where(index[j] == k, j, where)
        inverse.append(where)
    prod[touched] = jnp.zeros_like(prod[touched])

    for n, offset in enumerate(OFFSETS):
        @pl.when(jnp.logical_not(there(-offset)))
        def _():
            for slot in range(2):
                back[slot, n] = jnp.zeros_like(back[slot, n])
                halo[slot, 2 * (REACH - offset) : 2 * (REACH - offset) + 2] = jnp.zeros((2, 32, BR), F32)

    for i in range(6):
        loads[7 + i].wait()
        cut = pl.ds(rows * i, rows)
        high, low = split(s_full[cut])
        s_high[cut] = high
        s_low[cut] = low
    for copy in halo_copies:
        copy.wait_recv()
    picked, product = apply(0)
    put_parts(0, product)
    back_copies = send_back(0)
    hear(0)
    pass_on(1)
    pads_copy.wait_recv()
    mean_cond = 0.5 * (pad_out[0, 32:33] + pad_in[0, 32:33])
    image = collect(0, back_copies, mean_cond * (own_pads - pad_in[0, :32]))

    for i in range(2):
        image_own[i] = image[i]
        halo[1, 2 * REACH + i] = scale[i] * image[i]
    halo_copies = send_halo(1)
    own_pads = pads_of(1)
    pad_out[1, :32] = own_pads
    pads_copy = send_pads(1)
    moments = [jnp.zeros((32, BR), F32)] * 4
    for i in range(2):
        old, u = halo[0, 2 * REACH + i], halo[1, 2 * REACH + i]
        moments = [
            moments[0] + b_own[i] * old,
            moments[1] + old * image[i],
            moments[2] + u * image[i],
            moments[3] + leak[i] * u * u,
        ]
    pads_copy.wait_recv()
    coupling = mean_cond * (own_pads - pad_in[1, :32])
    moments[3] = moments[3] + own_pads * coupling
    for copy in halo_copies:
        copy.wait_recv()
    picked, product = apply(1)
    for j in range(touched):
        moments[3] = moments[3] + picked[j] * product[j]

    hear(1)

    group_a[a_id] = jnp.sum(jnp.concatenate(moments, axis=0).T, axis=0, keepdims=True)
    rows_a = spread_row(group_a, a_id, a_send, a_recv, [in_a(step) for step in order_a])
    put_parts(1, product)
    back_copies = send_back(1)
    rows_a.wait_recv()
    group_b[chip] = jnp.sum(group_a[...], axis=0)
    rows_b = spread_row(group_b, chip, b_send, b_recv, [in_b(step) for step in order_b])
    image_u = collect(1, back_copies, coupling)
    for copy in sent:
        copy.wait_send()
    rows_a.wait_send()
    rows_b.wait_recv()
    total = jnp.broadcast_to(jnp.sum(group_b[...], axis=0), (128, 128)).T
    m0, m1, m2, m3 = [total[32 * k : 32 * (k + 1)] for k in range(4)]
    alpha0 = m0 / m1
    cross = m1 - alpha0 * m2
    fresh = (m0 - alpha0 * m1) - alpha0 * cross
    beta = fresh / m0
    bend = cross - alpha0 * (m2 - alpha0 * m3)
    alpha1 = fresh / (bend + beta * (2.0 * cross + beta * m1))
    for i in range(2):
        old = halo[0, 2 * REACH + i]
        residual = b_own[i] - alpha0 * image_own[i]
        direction = scale[i] * residual + beta * old
        image1 = (image_own[i] - alpha0 * image_u[i]) + beta * image_own[i]
        x_out[0, :, BR * i : BR * (i + 1)] = alpha0 * old + alpha1 * direction
        r_out[0, :, BR * i : BR * (i + 1)] = residual - alpha1 * image1
    rows_b.wait_send()


def put_out(x_in, r_in, x_out, r_out, sem):
    copies = [
        pltpu.make_async_copy(x_in, x_out, sem.at[0]),
        pltpu.make_async_copy(r_in, r_out, sem.at[1]),
    ]
    for copy in copies:
        copy.start()
    for copy in copies:
        copy.wait()


def solution(mesh):
    n_board, n_sub = mesh.shape["board"], mesh.shape["sub"]
    vmem = pl.BlockSpec(memory_space=pltpu.VMEM)
    hbm = pl.BlockSpec(memory_space=pltpu.HBM)

    def on_device(rhs, schur, block_list, pad_rows, pad_cond, sink, precond):
        cases, owned = rhs.shape[1:]
        inner = schur.shape[1]
        n_off = len(OFFSETS)
        span = 2 * (2 * REACH + 1)
        dma = pltpu.SemaphoreType.DMA
        out = jax.ShapeDtypeStruct(rhs.shape, F32)
        results = pl.pallas_call(
            functools.partial(kernel, n_board, n_sub),
            out_shape=(out, out),
            in_specs=[hbm] * 7,
            out_specs=(vmem, vmem),
            scratch_shapes=[
                pltpu.SMEM(block_list.shape, jnp.int32),
                pltpu.VMEM(pad_rows.shape, jnp.int32),
                pltpu.VMEM(pad_cond.shape, F32),
                pltpu.VMEM(sink.shape, F32),
                pltpu.VMEM(precond.shape, F32),
                pltpu.VMEM((2, cases, BR), F32),
                pltpu.VMEM((inner, inner), F32),
                pltpu.VMEM((inner, inner), BF16),
                pltpu.VMEM((inner, inner), BF16),
                pltpu.VMEM((owned, BR), BF16),
                pltpu.VMEM((2, cases + 8, BR), F32),
                pltpu.VMEM((2, cases + 8, BR), F32),
                pltpu.VMEM((2, span, cases, BR), F32),
                pltpu.VMEM((block_list.shape[1] + 1, cases, BR), F32),
                pltpu.VMEM((2, span, cases, BR), F32),
                pltpu.VMEM((2, n_off, 2, cases, BR), F32),
                pltpu.VMEM((2, cases, BR), F32),
                pltpu.VMEM((2 * n_board, 1, 128), F32),
                pltpu.VMEM((n_sub // 2, 1, 128), F32),
                dma((13,)),
                dma((2, n_off)), dma((2, n_off)),
                dma((2, n_off)), dma((2, n_off)),
                dma((2,)), dma((2,)),
                dma(()), dma(()),
                dma(()), dma(()),
                pltpu.SemaphoreType.REGULAR((2,)),
            ],
            compiler_params=pltpu.CompilerParams(
                collective_id=0, has_side_effects=True, vmem_limit_bytes=32 * 1024 * 1024
            ),
        )(*[pltpu.with_memory_space_constraint(a, pltpu.HBM) for a in (rhs, schur, block_list, pad_rows, pad_cond, sink, precond)])
        return pl.pallas_call(
            put_out,
            out_shape=(out, out),
            in_specs=[vmem, vmem],
            out_specs=(hbm, hbm),
            scratch_shapes=[dma((2,))],
            compiler_params=pltpu.CompilerParams(vmem_limit_bytes=8 * 1024 * 1024),
        )(*results)

    row = P("board", "sub")
    return jax.shard_map(
        on_device,
        mesh=mesh,
        in_specs=(P("board", None, "sub"), P("board", "sub", None), row, row, row, row, row),
        out_specs=(P("board", None, "sub"), P("board", None, "sub")),
        check_vma=False,
    )
```

```python
import functools

import jax
import jax.numpy as jnp
from jax import lax
from jax.experimental import pallas as pl
from jax.experimental.pallas import tpu as pltpu
from jax.sharding import PartitionSpec as P

BR = 128
REACH = 3
HALF = 16
OFFSETS = (3, -3, 2, -2, 1, -1)
F32 = jnp.float32
BF16 = jnp.bfloat16


def split(value):
    high = value.astype(BF16)
    low = (value - high.astype(F32)).astype(BF16)
    return high, low


def bits(count):
    return count.bit_length() - 1


RING4 = (0, 1, 2, 1)
RING8 = (0, 1, 2, 2, 4, 3, 2, 2)


def far_first(count, hops):
    return sorted(range(1, count), key=lambda step: -hops(step))


class Copy:
    def __init__(self, copy, going, coming):
        self.copy, self.going, self.coming = copy, going, coming

    def when(self, condition, act):
        if condition is None:
            act()
        else:
            pl.when(condition)(act)

    def start(self):
        self.when(self.going, self.copy.start)

    def wait_recv(self):
        self.when(self.coming, self.copy.wait_recv)

    def wait_send(self):
        self.when(self.going, self.copy.wait_send)


def kernel(
    n_board, n_sub,
    rhs, schur, blocks_in, pad_rows_in, pad_cond_in, sink_in, precond_in,
    x_out, r_out,
    blocks, pad_rows, pad_cond, sink, precond,
    b_own, s_full, s_high, s_low, one_hot, pad_out, pad_in,
    halo_first, halo_second, prod, parts, back, image_own, group_a, group_b,
    load_sem, halo_send, halo_recv, back_send, back_recv, pad_send, pad_recv,
    a_send, a_recv, b_send, b_recv, relay,
):
    halo = (halo_first, halo_second)
    me_b = lax.axis_index("board")
    me_s = lax.axis_index("sub")
    core = lax.rem(me_s, 2)
    chip = lax.div(me_s, 2)
    n_a, n_chip = 2 * n_board, n_sub // 2
    a_id = me_b * 2 + core
    touched = blocks.shape[1]
    inner = schur.shape[1]
    order_a = far_first(n_a, lambda step: RING8[step // 2])
    order_b = far_first(n_chip, lambda step: RING4[step % 4] + RING8[step // 4])

    def near(offset):
        return (me_b, me_s + offset)

    def there(offset):
        if offset > 0:
            return me_s < n_sub - offset
        return me_s >= -offset

    flip_b = [(1 << k) * (1 - 2 * lax.rem(lax.div(me_b, 1 << k), 2)) for k in range(bits(n_board))]
    flip_s = [(1 << k) * (1 - 2 * lax.rem(lax.div(me_s, 1 << k), 2)) for k in range(bits(n_sub))]

    def flipped(me, flips, mask):
        for k, flip in enumerate(flips):
            if mask >> k & 1:
                me = me + flip
        return me

    def in_a(step):
        return (flipped(me_b, flip_b, step >> 1), flipped(me_s, flip_s, step & 1))

    def in_b(step):
        return (me_b, flipped(me_s, flip_s, 2 * step))

    def steps(count):
        return sorted({step % count for step in (1, -1, 2, -2)} - {0})

    layer = 8
    ring_b = [(lax.rem(me_b + step, n_board), me_s) for step in steps(n_board)]
    ring_s = [(me_b, lax.rem(me_s + layer * step, n_sub)) for step in steps(n_sub // layer)]
    row = [in_b(step) for step in range(1, layer // 2)]

    barrier = pltpu.get_barrier_semaphore()

    def greet(device):
        pl.semaphore_signal(barrier, inc=1, device_id=device, device_id_type=pl.DeviceIdType.MESH)

    count = len(ring_b) + len(ring_s) + len(row)
    for offset in OFFSETS:
        pl.when(there(offset))(lambda: greet(near(offset)))
        count = count + there(offset).astype(jnp.int32)
    for device in row + ring_b + ring_s:
        greet(device)

    loads = [
        pltpu.make_async_copy(rhs.at[0, :, pl.ds(BR * i, BR)], b_own.at[i], load_sem.at[i])
        for i in range(2)
    ]
    small = ((precond_in, precond), (pad_rows_in, pad_rows), (blocks_in, blocks), (pad_cond_in, pad_cond), (sink_in, sink))
    for i, (source, target) in enumerate(small):
        loads.append(pltpu.make_async_copy(source, target, load_sem.at[2 + i]))
    rows = inner // 6
    for i in range(6):
        cut = pl.ds(rows * i, rows)
        loads.append(pltpu.make_async_copy(schur.at[0, cut], s_full.at[cut], load_sem.at[7 + i]))
    for load in loads:
        load.start()

    for load in loads[:3]:
        load.wait()
    scale = [precond[0:1, BR * i : BR * (i + 1)] for i in range(2)]
    for i in range(2):
        for part in range(2):
            halo[part][0, 2 * REACH + i] = scale[i] * b_own[i, HALF * part : HALF * (part + 1)]
    pl.semaphore_wait(barrier, count)

    def pass_on(turn):
        for device in ring_b + ring_s:
            pl.semaphore_signal(relay.at[turn], inc=1, device_id=device, device_id_type=pl.DeviceIdType.MESH)

    def hear(turn):
        pl.semaphore_wait(relay.at[turn], len(ring_b) + len(ring_s))

    sent = []

    def send(source, target, send_sem, recv_sem, device, going=None, coming=None):
        copy = Copy(pltpu.make_async_remote_copy(
            src_ref=source, dst_ref=target, send_sem=send_sem, recv_sem=recv_sem,
            device_id=device, device_id_type=pl.DeviceIdType.MESH,
        ), going, coming)
        copy.start()
        sent.append(copy)
        return copy

    def spread_row(group, me, send_sem, recv_sem, devices):
        for device in devices:
            pltpu.make_async_remote_copy(
                src_ref=group.at[me], dst_ref=group.at[me], send_sem=send_sem, recv_sem=recv_sem,
                device_id=device, device_id_type=pl.DeviceIdType.MESH,
            ).start()
        others = group.at[pl.ds(0, len(devices))]
        return pltpu.make_async_remote_copy(
            src_ref=others, dst_ref=others, send_sem=send_sem, recv_sem=recv_sem,
            device_id=devices[0], device_id_type=pl.DeviceIdType.MESH,
        )

    def send_halo(slot, part):
        return [
            send(halo[part].at[slot, pl.ds(2 * REACH, 2)], halo[part].at[slot, pl.ds(2 * (REACH - offset), 2)],
                 halo_send.at[slot, part, n], halo_recv.at[slot, part, n], near(offset), there(offset), there(-offset))
            for n, offset in enumerate(OFFSETS)
        ]

    def send_pads(slot):
        return send(pad_out.at[slot], pad_in.at[slot], pad_send.at[slot], pad_recv.at[slot], in_a(2))

    def own(slot, i):
        return jnp.concatenate([halo[part][slot, 2 * REACH + i] for part in range(2)], axis=0)

    def pads_of(slot):
        high, low = split(jnp.concatenate([own(slot, 0), own(slot, 1)], axis=1))
        both = jnp.dot(jnp.concatenate([high, low], axis=0), one_hot[...], preferred_element_type=F32)
        return both[:32] + both[32:]

    def send_back(slot, part):
        return [
            send(parts.at[slot, part, pl.ds(2 * (REACH + offset), 2)], back.at[slot, part, n],
                 back_send.at[slot, part, n], back_recv.at[slot, part, n], near(offset), there(offset), there(-offset))
            for n, offset in enumerate(OFFSETS)
        ]

    def apply(slot, part):
        picked = [halo[part][slot, index[j]] for j in range(touched)]
        splits = [split(block) for block in picked]
        high = jnp.concatenate([pair[0] for pair in splits], axis=1)
        low = jnp.concatenate([pair[1] for pair in splits], axis=1)
        both = jnp.dot(jnp.concatenate([high, low], axis=0), s_high[...], preferred_element_type=F32)
        product = both[:HALF] + both[HALF:] + jnp.dot(high, s_low[...], preferred_element_type=F32)
        return picked, [product[:, BR * j : BR * (j + 1)] for j in range(touched)]

    def put_parts(slot, part, product):
        for j in range(touched):
            prod[part, j] = product[j]
        for k in range(2 * (2 * REACH + 1)):
            parts[slot, part, k] = prod[part, inverse[k]]

    def spread_pads(coupling):
        high, low = split(coupling)
        both = lax.dot_general(
            jnp.concatenate([high, low], axis=0), one_hot[...], (((1,), (1,)), ((), ())), preferred_element_type=F32)
        return both[:32] + both[32:]

    def collect(slot, part, copies, spread):
        cut = slice(HALF * part, HALF * (part + 1))
        for copy in copies:
            copy.wait_recv()
        result = []
        for i in range(2):
            total = parts[slot, part, 2 * REACH + i]
            for n in range(len(OFFSETS)):
                total = total + back[slot, part, n, i]
            total = total + spread[cut, BR * i : BR * (i + 1)]
            result.append(total + leak[i] * halo[part][slot, 2 * REACH + i])
        return result

    halo_copies = [send_halo(0, part) for part in range(2)]
    pass_on(0)
    for load in loads[3:7]:
        load.wait()
    leak = [sink[0:1, BR * i : BR * (i + 1)] for i in range(2)]
    n_pads = pad_rows.shape[1]
    row_ids = lax.broadcasted_iota(jnp.int32, (2 * BR, n_pads), 0)
    one_hot[...] = jnp.zeros_like(one_hot)
    one_hot[:, :n_pads] = jnp.where(row_ids == pad_rows[...], 1.0, 0.0).astype(BF16)
    own_pads = pads_of(0)
    pad_out[...] = jnp.zeros_like(pad_out)
    pad_out[0, :32] = own_pads
    pad_out[0, 32:33, :n_pads] = pad_cond[...]
    pads_copy = send_pads(0)
    last = 2 * (2 * REACH + 1) - 1
    index = [jnp.clip(blocks[0, j] - (me_s - REACH) * 2, 0, last) for j in range(touched)]
    inverse = []
    for k in range(last + 1):
        where = jnp.int32(touched)
        for j in range(touched):
            where = jnp.where(index[j] == k, j, where)
        inverse.append(where)
    for part in range(2):
        prod[part, touched] = jnp.zeros((HALF, BR), F32)

    for n, offset in enumerate(OFFSETS):
        @pl.when(jnp.logical_not(there(-offset)))
        def _():
            nothing = jnp.zeros((2, HALF, BR), F32)
            for slot in range(2):
                for part in range(2):
                    back[slot, part, n] = nothing
                    halo[part][slot, 2 * (REACH - offset) : 2 * (REACH - offset) + 2] = nothing

    for i in range(6):
        loads[7 + i].wait()
        cut = pl.ds(rows * i, rows)
        high, low = split(s_full[cut])
        s_high[cut] = high
        s_low[cut] = low
    back_copies = []
    for part in range(2):
        for copy in halo_copies[part]:
            copy.wait_recv()
        picked, product = apply(0, part)
        put_parts(0, part, product)
        back_copies.append(send_back(0, part))
    hear(0)
    pass_on(1)
    pads_copy.wait_recv()
    mean_cond = 0.5 * (pad_out[0, 32:33] + pad_in[0, 32:33])
    spread = spread_pads(mean_cond * (own_pads - pad_in[0, :32]))

    halo_copies = []
    for part in range(2):
        cut = slice(HALF * part, HALF * (part + 1))
        image = collect(0, part, back_copies[part], spread)
        for i in range(2):
            image_own[i, cut] = image[i]
            halo[part][1, 2 * REACH + i] = scale[i] * image[i]
        halo_copies.append(send_halo(1, part))
    own_pads = pads_of(1)
    pad_out[1, :32] = own_pads
    pads_copy = send_pads(1)
    moments = [jnp.zeros((32, BR), F32)] * 4
    for i in range(2):
        old, u = own(0, i), own(1, i)
        moments = [
            moments[0] + b_own[i] * old,
            moments[1] + old * image_own[i],
            moments[2] + u * image_own[i],
            moments[3] + leak[i] * u * u,
        ]
    pads_copy.wait_recv()
    coupling = mean_cond * (own_pads - pad_in[1, :32])
    moments[3] = moments[3] + own_pads * coupling
    products, inner_parts = [], []
    for part in range(2):
        for copy in halo_copies[part]:
            copy.wait_recv()
        picked, product = apply(1, part)
        products.append(product)
        inner_parts.append(sum(picked[j] * product[j] for j in range(touched)))
    moments[3] = moments[3] + jnp.concatenate(inner_parts, axis=0)
    hear(1)

    group_a[a_id] = jnp.sum(jnp.concatenate(moments, axis=0).T, axis=0, keepdims=True)
    rows_a = spread_row(group_a, a_id, a_send, a_recv, [in_a(step) for step in order_a])
    back_copies = []
    for part in range(2):
        put_parts(1, part, products[part])
        back_copies.append(send_back(1, part))
    rows_a.wait_recv()
    group_b[chip] = jnp.sum(group_a[...], axis=0)
    rows_b = spread_row(group_b, chip, b_send, b_recv, [in_b(step) for step in order_b])
    spread = spread_pads(coupling)
    halves = [collect(1, part, back_copies[part], spread) for part in range(2)]
    image_u = [jnp.concatenate([half[i] for half in halves], axis=0) for i in range(2)]
    for copy in sent:
        copy.wait_send()
    rows_a.wait_send()
    rows_b.wait_recv()
    total = jnp.broadcast_to(jnp.sum(group_b[...], axis=0), (128, 128)).T
    m0, m1, m2, m3 = [total[32 * k : 32 * (k + 1)] for k in range(4)]
    alpha0 = m0 / m1
    cross = m1 - alpha0 * m2
    fresh = (m0 - alpha0 * m1) - alpha0 * cross
    beta = fresh / m0
    bend = cross - alpha0 * (m2 - alpha0 * m3)
    alpha1 = fresh / (bend + beta * (2.0 * cross + beta * m1))
    for i in range(2):
        old = own(0, i)
        residual = b_own[i] - alpha0 * image_own[i]
        direction = scale[i] * residual + beta * old
        image1 = (image_own[i] - alpha0 * image_u[i]) + beta * image_own[i]
        x_out[0, :, BR * i : BR * (i + 1)] = alpha0 * old + alpha1 * direction
        r_out[0, :, BR * i : BR * (i + 1)] = residual - alpha1 * image1
    rows_b.wait_send()


def put_out(x_in, r_in, x_out, r_out, sem):
    copies = [
        pltpu.make_async_copy(x_in, x_out, sem.at[0]),
        pltpu.make_async_copy(r_in, r_out, sem.at[1]),
    ]
    for copy in copies:
        copy.start()
    for copy in copies:
        copy.wait()


def solution(mesh):
    n_board, n_sub = mesh.shape["board"], mesh.shape["sub"]
    vmem = pl.BlockSpec(memory_space=pltpu.VMEM)
    hbm = pl.BlockSpec(memory_space=pltpu.HBM)

    def on_device(rhs, schur, block_list, pad_rows, pad_cond, sink, precond):
        cases, owned = rhs.shape[1:]
        inner = schur.shape[1]
        n_off = len(OFFSETS)
        span = 2 * (2 * REACH + 1)
        dma = pltpu.SemaphoreType.DMA
        out = jax.ShapeDtypeStruct(rhs.shape, F32)
        results = pl.pallas_call(
            functools.partial(kernel, n_board, n_sub),
            out_shape=(out, out),
            in_specs=[hbm] * 7,
            out_specs=(vmem, vmem),
            scratch_shapes=[
                pltpu.SMEM(block_list.shape, jnp.int32),
                pltpu.VMEM(pad_rows.shape, jnp.int32),
                pltpu.VMEM(pad_cond.shape, F32),
                pltpu.VMEM(sink.shape, F32),
                pltpu.VMEM(precond.shape, F32),
                pltpu.VMEM((2, cases, BR), F32),
                pltpu.VMEM((inner, inner), F32),
                pltpu.VMEM((inner, inner), BF16),
                pltpu.VMEM((inner, inner), BF16),
                pltpu.VMEM((owned, BR), BF16),
                pltpu.VMEM((2, cases + 8, BR), F32),
                pltpu.VMEM((2, cases + 8, BR), F32),
                pltpu.VMEM((2, span, HALF, BR), F32),
                pltpu.VMEM((2, span, HALF, BR), F32),
                pltpu.VMEM((2, block_list.shape[1] + 1, HALF, BR), F32),
                pltpu.VMEM((2, 2, span, HALF, BR), F32),
                pltpu.VMEM((2, 2, n_off, 2, HALF, BR), F32),
                pltpu.VMEM((2, cases, BR), F32),
                pltpu.VMEM((2 * n_board, 1, 128), F32),
                pltpu.VMEM((n_sub // 2, 1, 128), F32),
                dma((13,)),
                dma((2, 2, n_off)), dma((2, 2, n_off)),
                dma((2, 2, n_off)), dma((2, 2, n_off)),
                dma((2,)), dma((2,)),
                dma(()), dma(()),
                dma(()), dma(()),
                pltpu.SemaphoreType.REGULAR((2,)),
            ],
            compiler_params=pltpu.CompilerParams(
                collective_id=0, has_side_effects=True, vmem_limit_bytes=32 * 1024 * 1024
            ),
        )(*[pltpu.with_memory_space_constraint(a, pltpu.HBM) for a in (rhs, schur, block_list, pad_rows, pad_cond, sink, precond)])
        return pl.pallas_call(
            put_out,
            out_shape=(out, out),
            in_specs=[vmem, vmem],
            out_specs=(hbm, hbm),
            scratch_shapes=[dma((2,))],
            compiler_params=pltpu.CompilerParams(vmem_limit_bytes=8 * 1024 * 1024),
        )(*results)

    row = P("board", "sub")
    return jax.shard_map(
        on_device,
        mesh=mesh,
        in_specs=(P("board", None, "sub"), P("board", "sub", None), row, row, row, row, row),
        out_specs=(P("board", None, "sub"), P("board", None, "sub")),
        check_vma=False,
    )
```

```python
import functools

import jax
import jax.numpy as jnp
from jax import lax
from jax.experimental import pallas as pl
from jax.experimental.pallas import tpu as pltpu
from jax.sharding import PartitionSpec as P

BR = 128
REACH = 3
HALF = 16
OFFSETS = (3, -3, 2, -2, 1, -1)
F32 = jnp.float32
BF16 = jnp.bfloat16


def split(value):
    high = value.astype(BF16)
    low = (value - high.astype(F32)).astype(BF16)
    return high, low


def bits(count):
    return count.bit_length() - 1


RING4 = (0, 1, 2, 1)
RING8 = (0, 1, 2, 2, 4, 3, 2, 2)


def far_first(count, hops):
    return sorted(range(1, count), key=lambda step: -hops(step))


class Copy:
    def __init__(self, copy, going, coming):
        self.copy, self.going, self.coming = copy, going, coming

    def when(self, condition, act):
        if condition is None:
            act()
        else:
            pl.when(condition)(act)

    def start(self):
        self.when(self.going, self.copy.start)

    def wait_recv(self):
        self.when(self.coming, self.copy.wait_recv)

    def wait_send(self):
        self.when(self.going, self.copy.wait_send)


def kernel(
    n_board, n_sub,
    rhs, schur, blocks_in, pad_rows_in, pad_cond_in, sink_in, precond_in,
    x_out, r_out,
    blocks, pad_rows, pad_cond, sink, precond,
    b_own, s_full, s_high, s_low, one_hot, pad_out, pad_in,
    halo_first, halo_second, prod, parts, back, image_own, group_a, group_b,
    load_sem, halo_send, halo_recv, back_send, back_recv, pad_send, pad_recv,
    a_send, a_recv, b_send, b_recv, relay,
):
    halo = (halo_first, halo_second)
    me_b = lax.axis_index("board")
    me_s = lax.axis_index("sub")
    core = lax.rem(me_s, 2)
    chip = lax.div(me_s, 2)
    n_a, n_chip = 2 * n_board, n_sub // 2
    a_id = me_b * 2 + core
    touched = blocks.shape[1]
    inner = schur.shape[1]
    order_a = far_first(n_a, lambda step: RING8[step // 2])
    order_b = far_first(n_chip, lambda step: RING4[step % 4] + RING8[step // 4])

    def near(offset):
        return (me_b, me_s + offset)

    def there(offset):
        if offset > 0:
            return me_s < n_sub - offset
        return me_s >= -offset

    flip_b = [(1 << k) * (1 - 2 * lax.rem(lax.div(me_b, 1 << k), 2)) for k in range(bits(n_board))]
    flip_s = [(1 << k) * (1 - 2 * lax.rem(lax.div(me_s, 1 << k), 2)) for k in range(bits(n_sub))]

    def flipped(me, flips, mask):
        for k, flip in enumerate(flips):
            if mask >> k & 1:
                me = me + flip
        return me

    def in_a(step):
        return (flipped(me_b, flip_b, step >> 1), flipped(me_s, flip_s, step & 1))

    def in_b(step):
        return (me_b, flipped(me_s, flip_s, 2 * step))

    def steps(count):
        return sorted({step % count for step in (1, -1, 2, -2)} - {0})

    layer = 8
    ring_b = [(lax.rem(me_b + step, n_board), me_s) for step in steps(n_board)]
    ring_s = [(me_b, lax.rem(me_s + layer * step, n_sub)) for step in steps(n_sub // layer)]
    row = [in_b(step) for step in range(1, layer // 2)]

    barrier = pltpu.get_barrier_semaphore()

    def greet(device):
        pl.semaphore_signal(barrier, inc=1, device_id=device, device_id_type=pl.DeviceIdType.MESH)

    count = len(ring_b) + len(ring_s) + len(row)
    for offset in OFFSETS:
        pl.when(there(offset))(lambda: greet(near(offset)))
        count = count + there(offset).astype(jnp.int32)
    for device in row + ring_b + ring_s:
        greet(device)

    loads = [
        pltpu.make_async_copy(rhs.at[0, :, pl.ds(BR * i, BR)], b_own.at[i], load_sem.at[i])
        for i in range(2)
    ]
    small = ((precond_in, precond), (pad_rows_in, pad_rows), (blocks_in, blocks), (pad_cond_in, pad_cond), (sink_in, sink))
    for i, (source, target) in enumerate(small):
        loads.append(pltpu.make_async_copy(source, target, load_sem.at[2 + i]))
    rows = inner // 6
    for i in range(6):
        cut = pl.ds(rows * i, rows)
        loads.append(pltpu.make_async_copy(schur.at[0, cut], s_full.at[cut], load_sem.at[7 + i]))
    for load in loads:
        load.start()

    for load in loads[:3]:
        load.wait()
    scale = [precond[0:1, BR * i : BR * (i + 1)] for i in range(2)]
    for i in range(2):
        for part in range(2):
            halo[part][0, 2 * REACH + i] = scale[i] * b_own[i, HALF * part : HALF * (part + 1)]
    pl.semaphore_wait(barrier, count)

    def pass_on(turn):
        for device in ring_b + ring_s:
            pl.semaphore_signal(relay.at[turn], inc=1, device_id=device, device_id_type=pl.DeviceIdType.MESH)

    def hear(turn):
        pl.semaphore_wait(relay.at[turn], len(ring_b) + len(ring_s))

    sent = []

    def send(source, target, send_sem, recv_sem, device, going=None, coming=None):
        copy = Copy(pltpu.make_async_remote_copy(
            src_ref=source, dst_ref=target, send_sem=send_sem, recv_sem=recv_sem,
            device_id=device, device_id_type=pl.DeviceIdType.MESH,
        ), going, coming)
        copy.start()
        sent.append(copy)
        return copy

    def spread_row(group, me, send_sem, recv_sem, devices):
        for device in devices:
            pltpu.make_async_remote_copy(
                src_ref=group.at[pl.ds(me, 1)], dst_ref=group.at[pl.ds(me, 1)], send_sem=send_sem, recv_sem=recv_sem,
                device_id=device, device_id_type=pl.DeviceIdType.MESH,
            ).start()
        others = group.at[pl.ds(0, len(devices))]
        return pltpu.make_async_remote_copy(
            src_ref=others, dst_ref=others, send_sem=send_sem, recv_sem=recv_sem,
            device_id=devices[0], device_id_type=pl.DeviceIdType.MESH,
        )

    def send_halo(slot, part):
        return [
            send(halo[part].at[slot, pl.ds(2 * REACH, 2)], halo[part].at[slot, pl.ds(2 * (REACH - offset), 2)],
                 halo_send.at[slot, part, n], halo_recv.at[slot, part, n], near(offset), there(offset), there(-offset))
            for n, offset in enumerate(OFFSETS)
        ]

    def send_pads(slot):
        return send(pad_out.at[slot], pad_in.at[slot], pad_send.at[slot], pad_recv.at[slot], in_a(2))

    def own(slot, i):
        return jnp.concatenate([halo[part][slot, 2 * REACH + i] for part in range(2)], axis=0)

    def pads_of(slot):
        high, low = split(jnp.concatenate([own(slot, 0), own(slot, 1)], axis=1))
        both = jnp.dot(jnp.concatenate([high, low], axis=0), one_hot[...], preferred_element_type=F32)
        return both[:32] + both[32:]

    def send_back(slot, part):
        return [
            send(parts.at[slot, part, pl.ds(2 * (REACH + offset), 2)], back.at[slot, part, n],
                 back_send.at[slot, part, n], back_recv.at[slot, part, n], near(offset), there(offset), there(-offset))
            for n, offset in enumerate(OFFSETS)
        ]

    def apply(slot, part):
        picked = [halo[part][slot, index[j]] for j in range(touched)]
        splits = [split(block) for block in picked]
        high = jnp.concatenate([pair[0] for pair in splits], axis=1)
        low = jnp.concatenate([pair[1] for pair in splits], axis=1)
        both = jnp.dot(jnp.concatenate([high, low], axis=0), s_high[...], preferred_element_type=F32)
        product = both[:HALF] + both[HALF:] + jnp.dot(high, s_low[...], preferred_element_type=F32)
        return picked, [product[:, BR * j : BR * (j + 1)] for j in range(touched)]

    def put_parts(slot, part, product):
        for j in range(touched):
            prod[part, j] = product[j]
        for k in range(2 * (2 * REACH + 1)):
            parts[slot, part, k] = prod[part, inverse[k]]

    def spread_pads(coupling):
        high, low = split(coupling)
        both = lax.dot_general(
            jnp.concatenate([high, low], axis=0), one_hot[...], (((1,), (1,)), ((), ())), preferred_element_type=F32)
        return both[:32] + both[32:]

    def collect(slot, part, copies, spread):
        cut = slice(HALF * part, HALF * (part + 1))
        for copy in copies:
            copy.wait_recv()
        result = []
        for i in range(2):
            total = parts[slot, part, 2 * REACH + i]
            for n in range(len(OFFSETS)):
                total = total + back[slot, part, n, i]
            total = total + spread[cut, BR * i : BR * (i + 1)]
            result.append(total + leak[i] * halo[part][slot, 2 * REACH + i])
        return result

    halo_copies = [send_halo(0, part) for part in range(2)]
    pass_on(0)
    for load in loads[3:7]:
        load.wait()
    leak = [sink[0:1, BR * i : BR * (i + 1)] for i in range(2)]
    n_pads = pad_rows.shape[1]
    row_ids = lax.broadcasted_iota(jnp.int32, (2 * BR, n_pads), 0)
    one_hot[...] = jnp.zeros_like(one_hot)
    one_hot[:, :n_pads] = jnp.where(row_ids == pad_rows[...], 1.0, 0.0).astype(BF16)
    own_pads = pads_of(0)
    pad_out[...] = jnp.zeros_like(pad_out)
    pad_out[0, :32] = own_pads
    pad_out[0, 32:33, :n_pads] = pad_cond[...]
    pads_copy = send_pads(0)
    last = 2 * (2 * REACH + 1) - 1
    index = [jnp.clip(blocks[0, j] - (me_s - REACH) * 2, 0, last) for j in range(touched)]
    inverse = []
    for k in range(last + 1):
        where = jnp.int32(touched)
        for j in range(touched):
            where = jnp.where(index[j] == k, j, where)
        inverse.append(where)
    for part in range(2):
        prod[part, touched] = jnp.zeros((HALF, BR), F32)

    for n, offset in enumerate(OFFSETS):
        @pl.when(jnp.logical_not(there(-offset)))
        def _():
            nothing = jnp.zeros((2, HALF, BR), F32)
            for slot in range(2):
                for part in range(2):
                    back[slot, part, n] = nothing
                    halo[part][slot, 2 * (REACH - offset) : 2 * (REACH - offset) + 2] = nothing

    for i in range(6):
        loads[7 + i].wait()
        cut = pl.ds(rows * i, rows)
        high, low = split(s_full[cut])
        s_high[cut] = high
        s_low[cut] = low
    back_copies = []
    for part in range(2):
        for copy in halo_copies[part]:
            copy.wait_recv()
        picked, product = apply(0, part)
        put_parts(0, part, product)
        back_copies.append(send_back(0, part))
    hear(0)
    pass_on(1)
    pads_copy.wait_recv()
    mean_cond = 0.5 * (pad_out[0, 32:33] + pad_in[0, 32:33])
    spread = spread_pads(mean_cond * (own_pads - pad_in[0, :32]))

    halo_copies = []
    for part in range(2):
        cut = slice(HALF * part, HALF * (part + 1))
        image = collect(0, part, back_copies[part], spread)
        for i in range(2):
            image_own[i, cut] = image[i]
            halo[part][1, 2 * REACH + i] = scale[i] * image[i]
        halo_copies.append(send_halo(1, part))
    own_pads = pads_of(1)
    pad_out[1, :32] = own_pads
    pads_copy = send_pads(1)
    moments = [jnp.zeros((32, BR), F32)] * 4
    for i in range(2):
        old, u = own(0, i), own(1, i)
        moments = [
            moments[0] + b_own[i] * old,
            moments[1] + old * image_own[i],
            moments[2] + u * image_own[i],
            moments[3] + leak[i] * u * u,
        ]
    pads_copy.wait_recv()
    coupling = mean_cond * (own_pads - pad_in[1, :32])
    moments[3] = moments[3] + own_pads * coupling
    products, inner_parts = [], []
    for part in range(2):
        for copy in halo_copies[part]:
            copy.wait_recv()
        picked, product = apply(1, part)
        products.append(product)
        inner_parts.append(sum(picked[j] * product[j] for j in range(touched)))
    moments[3] = moments[3] + jnp.concatenate(inner_parts, axis=0)
    hear(1)

    group_a[pl.ds(a_id, 1)] = jnp.sum(jnp.concatenate(moments, axis=0).T, axis=0, keepdims=True)
    rows_a = spread_row(group_a, a_id, a_send, a_recv, [in_a(step) for step in order_a])
    back_copies = []
    for part in range(2):
        put_parts(1, part, products[part])
        back_copies.append(send_back(1, part))
    rows_a.wait_recv()
    group_b[pl.ds(chip, 1)] = jnp.sum(group_a[...], axis=0, keepdims=True)
    rows_b = spread_row(group_b, chip, b_send, b_recv, [in_b(step) for step in order_b])
    spread = spread_pads(coupling)
    halves = [collect(1, part, back_copies[part], spread) for part in range(2)]
    image_u = [jnp.concatenate([half[i] for half in halves], axis=0) for i in range(2)]
    for copy in sent:
        copy.wait_send()
    rows_a.wait_send()
    rows_b.wait_recv()
    total = jnp.broadcast_to(jnp.sum(group_b[...], axis=0, keepdims=True), (128, 128)).T
    m0, m1, m2, m3 = [total[32 * k : 32 * (k + 1)] for k in range(4)]
    alpha0 = m0 / m1
    cross = m1 - alpha0 * m2
    fresh = (m0 - alpha0 * m1) - alpha0 * cross
    beta = fresh / m0
    bend = cross - alpha0 * (m2 - alpha0 * m3)
    alpha1 = fresh / (bend + beta * (2.0 * cross + beta * m1))
    for i in range(2):
        old = own(0, i)
        residual = b_own[i] - alpha0 * image_own[i]
        direction = scale[i] * residual + beta * old
        image1 = (image_own[i] - alpha0 * image_u[i]) + beta * image_own[i]
        x_out[0, :, BR * i : BR * (i + 1)] = alpha0 * old + alpha1 * direction
        r_out[0, :, BR * i : BR * (i + 1)] = residual - alpha1 * image1
    rows_b.wait_send()


def put_out(x_in, r_in, x_out, r_out, sem):
    copies = [
        pltpu.make_async_copy(x_in, x_out, sem.at[0]),
        pltpu.make_async_copy(r_in, r_out, sem.at[1]),
    ]
    for copy in copies:
        copy.start()
    for copy in copies:
        copy.wait()


def solution(mesh):
    n_board, n_sub = mesh.shape["board"], mesh.shape["sub"]
    vmem = pl.BlockSpec(memory_space=pltpu.VMEM)
    hbm = pl.BlockSpec(memory_space=pltpu.HBM)

    def on_device(rhs, schur, block_list, pad_rows, pad_cond, sink, precond):
        cases, owned = rhs.shape[1:]
        inner = schur.shape[1]
        n_off = len(OFFSETS)
        span = 2 * (2 * REACH + 1)
        dma = pltpu.SemaphoreType.DMA
        out = jax.ShapeDtypeStruct(rhs.shape, F32)
        results = pl.pallas_call(
            functools.partial(kernel, n_board, n_sub),
            out_shape=(out, out),
            in_specs=[hbm] * 7,
            out_specs=(vmem, vmem),
            scratch_shapes=[
                pltpu.SMEM(block_list.shape, jnp.int32),
                pltpu.VMEM(pad_rows.shape, jnp.int32),
                pltpu.VMEM(pad_cond.shape, F32),
                pltpu.VMEM(sink.shape, F32),
                pltpu.VMEM(precond.shape, F32),
                pltpu.VMEM((2, cases, BR), F32),
                pltpu.VMEM((inner, inner), F32),
                pltpu.VMEM((inner, inner), BF16),
                pltpu.VMEM((inner, inner), BF16),
                pltpu.VMEM((owned, BR), BF16),
                pltpu.VMEM((2, cases + 8, BR), F32),
                pltpu.VMEM((2, cases + 8, BR), F32),
                pltpu.VMEM((2, span, HALF, BR), F32),
                pltpu.VMEM((2, span, HALF, BR), F32),
                pltpu.VMEM((2, block_list.shape[1] + 1, HALF, BR), F32),
                pltpu.VMEM((2, 2, span, HALF, BR), F32),
                pltpu.VMEM((2, 2, n_off, 2, HALF, BR), F32),
                pltpu.VMEM((2, cases, BR), F32),
                pltpu.VMEM((2 * n_board, 128), F32),
                pltpu.VMEM((n_sub // 2, 128), F32),
                dma((13,)),
                dma((2, 2, n_off)), dma((2, 2, n_off)),
                dma((2, 2, n_off)), dma((2, 2, n_off)),
                dma((2,)), dma((2,)),
                dma(()), dma(()),
                dma(()), dma(()),
                pltpu.SemaphoreType.REGULAR((2,)),
            ],
            compiler_params=pltpu.CompilerParams(
                collective_id=0, has_side_effects=True, vmem_limit_bytes=32 * 1024 * 1024
            ),
        )(*[pltpu.with_memory_space_constraint(a, pltpu.HBM) for a in (rhs, schur, block_list, pad_rows, pad_cond, sink, precond)])
        return pl.pallas_call(
            put_out,
            out_shape=(out, out),
            in_specs=[vmem, vmem],
            out_specs=(hbm, hbm),
            scratch_shapes=[dma((2,))],
            compiler_params=pltpu.CompilerParams(vmem_limit_bytes=8 * 1024 * 1024),
        )(*results)

    row = P("board", "sub")
    return jax.shard_map(
        on_device,
        mesh=mesh,
        in_specs=(P("board", None, "sub"), P("board", "sub", None), row, row, row, row, row),
        out_specs=(P("board", None, "sub"), P("board", None, "sub")),
        check_vma=False,
    )
```
